256 devices in a mesh: comp: 2 (over core), gx: 8 (over y, z_lo), gy: 16 (over x, z_hi).
Axes of the slice: x: 4, y: 4, z: 8 (z_hi: 4, z_lo: 2; z = z_hi * 2 + z_lo), core: 2. Of those that a mesh axis runs over, the one named last changes fastest.
Arguments:
- state_incr: float32 [2, 2, 128, 128, 2048], P('comp', None, None, 'gx', 'gy'), may hold values from -6 to 6
- winds: float32 [2, 2, 128, 128, 2048], P('comp', None, None, 'gx', 'gy'), may hold values from -0.4 to 0.4
- coupling: float32 [128, 2048], P('gx', 'gy'), may hold values from 0.1 to 0.6
- background: float32 [2, 2, 128], P('comp'), may hold values from 0.5 to 2
- obs_dest: int32 [131072, 1], P(('comp', 'gx', 'gy')), may hold values from 0 to 127; in each aligned block of 512 rows (0 to 511, 512 to 1023, ...) at most 8 rows name the same one
- obs_col: int32 [131072], P(('comp', 'gx', 'gy')), may hold values from 0 to 2047
- obs_op: float32 [131072, 256], P(('comp', 'gx', 'gy')), may hold values from -0.375 to 0.375
- obs_prec: float32 [131072], P(('comp', 'gx', 'gy')), may hold values from 0.5 to 4
Outputs:
- hess_vec: float32 [2, 2, 128, 128, 2048], P('comp', None, None, 'gx', 'gy')
The draws below stay inside these ranges and needn't reach their ends.
Inputs may be any that keep to these rules, and one draw needn't show every extreme that they name: `obs_dest`: among the rows of one device at most 8 name the same owner, a bound that some block reaches of them; owners are tiles of the record's own component. `obs_col`: column m of a tile is its cell (m // 128, m % 128).
All inputs are finite; a program needn't handle non-finite values.
Results may differ from the reference program's by a relative error of at most 0.000057.
Values sent between devices are 32-bit elements; how exact they have to be, the bound alone decides.
A program may use at most 128 MiB of HBM per device.

```python
import math
import jax
import jax.numpy as jnp
import numpy as np
from jax import lax

CX = 16
CY = 128
L = 128
OBS_DEV = 512
NX = 128
NY = 2048
OBS_CAP = 8
OBS_ALL = 131072
N_GX = 8
N_GY = 16


def place_ends(values, key, low, high):
    extent = values.shape
    spot = [jax.random.randint(jax.random.fold_in(key, axis), (), 0, extent[axis]) for axis in range(len(extent))]
    values = values.at[tuple(spot)].set(low)
    longest = extent.index(max(extent))
    spot[longest] = (spot[longest] + 1) % extent[longest]
    return values.at[tuple(spot)].set(high)


def level_of(rng, shape, shards, low, high):
    def one(axis_at, shards_of):
        draws = jax.random.uniform(jax.random.fold_in(jax.random.fold_in(rng, 6), axis_at), (shards_of,), jnp.float32, low / len(shards), high / len(shards))
        return jnp.repeat(jnp.exp(draws), shape[axis_at] // shards_of).reshape((-1,) + (1,) * (len(shape) - axis_at - 1))

    gain = one(*shards[0])
    for cut in shards[1:]:
        gain = gain * one(*cut)
    return gain


def routed_block(own_key, own, number, rows, number_of, top, bound, slope):
    ranking = jax.random.permutation(own_key, number_of)
    heavy_load, ordinary = shares(number_of, rows * top, bound, slope, True), shares(number_of, rows * top, bound, slope, False)
    places = jnp.arange(number_of)

    def named(tallies, offset_by):
        used = int((tallies > 0).sum())
        fixed = max(1, used // 4)
        moved = fixed + (places - fixed + offset_by * (used - fixed)) % max(1, number_of - fixed)
        return jnp.zeros((number_of,), jnp.int32).at[ranking[jnp.where(places < fixed, places, moved)]].set(jnp.asarray(tallies, jnp.int32))

    tallies = jnp.where(number % 4 == 0, named(heavy_load, number // 4), named(ordinary, number - number // 4 - 1))
    mixed = jax.random.permutation(jax.random.fold_in(own, 3), number_of)
    giver, receiver = mixed[0:number_of // 2 * 2:2], mixed[1:number_of // 2 * 2:2]
    margin = jnp.minimum(tallies[giver] - 1, bound - tallies[receiver]) // 2
    margin = jnp.where((giver == ranking[0]) | (receiver == ranking[0]) | (tallies[receiver] == 0), 0, jnp.maximum(margin, 0))
    moved = jax.random.randint(jax.random.fold_in(own, 4), (number_of // 2,), 0, 1 << 20) % (margin + 1)
    tallies = tallies.at[giver].add(-moved).at[receiver].add(moved)
    labels = jnp.searchsorted(jnp.cumsum(tallies), jnp.arange(rows * top), side="right").astype(jnp.int32)
    listing = labels.reshape(top, rows).T
    listing = listing[jax.random.permutation(jax.random.fold_in(own, 1), rows)]
    offset_by = jax.random.randint(jax.random.fold_in(own, 2), (rows, 1), 0, top)
    return jnp.take_along_axis(listing, (jnp.arange(top)[None, :] + offset_by) % top, axis=1)


def shares(number_of, total, most, lean, full):
    loads = [(1 << 20) // math.isqrt(standing ** lean) + 1 for standing in range(1, number_of + 1)]
    largest = most if full else min(most, max(-(-total // number_of), total * loads[0] // sum(loads)))
    least = 1 if total - largest >= number_of - 1 else 0
    counts, surplus = [largest] + [least] * (number_of - 1), total - largest - least * (number_of - 1)
    while surplus > 0:
        movable = [i for i in range(1, number_of) if counts[i] < largest] or [i for i in range(1, number_of) if counts[i] < most]
        pool, left = sum([loads[i] for i in movable]), surplus
        for i in movable:
            more = min(most - counts[i], max(1, left * loads[i] // pool), surplus)
            counts[i] = counts[i] + more
            surplus = surplus - more
    return np.array(counts)


def centred(stream_key, dims, scale, most, shards=(), kind=jnp.bfloat16):
    array = jax.random.normal(stream_key, dims, jnp.float32) * scale
    if len(shards) > 0:
        array = level_of(stream_key, dims, shards, -0.22, 0.18) * array
    return jnp.clip(array, min=-most, max=most).astype(kind)


def setup_inputs(seed: int = 0) -> dict:
    keys = jax.random.split(jax.random.key(seed), 9)
    state_incr = centred(keys[0], (2, 2, L, NX, NY), 1.0, 6.0, ((0, 2), (3, 8), (4, 16)), jnp.float32)
    winds = jnp.clip(jax.random.uniform(keys[1], (2, 2, L, NX, NY), jnp.float32, -0.4, 0.4) * level_of(keys[1], (2, 2, L, NX, NY), ((0, 2), (3, 8), (4, 16)), -0.4, 0.0), -0.4, 0.4)
    coupling = jnp.clip(jnp.exp(math.log(0.6) - 1.7917595 * jax.random.uniform(keys[2], (NX, NY), jnp.float32) ** level_of(keys[2], (NX, NY), ((0, 8), (1, 16)), -0.2, 0.2)), 0.1, 0.6)
    background = jnp.clip(jnp.exp(math.log(2.0) - 1.3862944 * jax.random.uniform(keys[3], (2, 2, L), jnp.float32) ** level_of(keys[3], (2, 2, L), ((0, 2),), -0.2, 0.2)), 0.5, 2.0)
    obs_dest_keys = jax.random.split(jax.random.fold_in(keys[4], 1), OBS_ALL // OBS_DEV)
    obs_dest_turns = jax.random.permutation(jax.random.fold_in(keys[4], 3), OBS_ALL // OBS_DEV)
    obs_dest = jax.vmap(lambda own, number: routed_block(jax.random.fold_in(keys[4], 2), own, number, OBS_DEV, N_GX * N_GY, 1, OBS_CAP, 2))(obs_dest_keys, obs_dest_turns).reshape((OBS_ALL, 1))
    obs_col = place_ends(jax.random.randint(keys[5], (OBS_ALL,), 0, CX * CY), jax.random.fold_in(keys[5], 1), 0, (CX * CY) - 1).astype(jnp.int32)
    obs_op = centred(keys[6], (OBS_ALL, 2 * L), (2 * L) ** -0.5, 0.375, ((0, 256),), jnp.float32)
    obs_prec = jnp.clip(jnp.exp(math.log(4.0) - 2.0794415 * jax.random.uniform(keys[7], (OBS_ALL,), jnp.float32) ** level_of(keys[7], (OBS_ALL,), ((0, 256),), -0.2, 0.2)), 0.5, 4.0)
    return dict(state_incr=state_incr, winds=winds, coupling=coupling, background=background, obs_dest=obs_dest, obs_col=obs_col, obs_op=obs_op, obs_prec=obs_prec)


HORIZ_MIX = 0.1
VERT_MIX = 0.15

def vertical(field):
    upper = jnp.concatenate([field[:, :, 1:], field[:, :, -1:]], axis=2)
    lower = jnp.concatenate([field[:, :, :1], field[:, :, :-1]], axis=2)
    return VERT_MIX * (upper + lower - 2.0 * field)

def stencil(field, wind_x, wind_y):
    padded = jnp.pad(field, ((0, 0), (0, 0), (0, 0), (1, 1), (1, 1)))
    wind_x = wind_x[:, None]
    wind_y = wind_y[:, None]
    result = field * (1.0 - 4.0 * HORIZ_MIX) + vertical(field)
    result = result + (HORIZ_MIX - 0.5 * wind_x) * padded[:, :, :, 2:, 1:-1]
    result = result + (HORIZ_MIX + 0.5 * wind_x) * padded[:, :, :, :-2, 1:-1]
    result = result + (HORIZ_MIX - 0.5 * wind_y) * padded[:, :, :, 1:-1, 2:]
    result = result + (HORIZ_MIX + 0.5 * wind_y) * padded[:, :, :, 1:-1, :-2]
    return result

def couple(field, coupling):
    atmos = field[0, :, 0]
    ocean = field[1, :, 0]
    atmos_new = atmos - coupling * (atmos - ocean)
    ocean_new = ocean - 0.5 * coupling * (ocean - atmos)
    return field.at[0, :, 0].set(atmos_new).at[1, :, 0].set(ocean_new)

def reference(state_incr, winds, coupling, background, obs_dest, obs_col, obs_op, obs_prec):
    wind_x = winds[:, 0]
    wind_y = winds[:, 1]

    def tangent(field):
        for sweep in range(2):
            field = couple(stencil(field, wind_x, wind_y), coupling)
        return field
    second, pullback = jax.vjp(tangent, state_incr)
    record_ids = jnp.arange(OBS_ALL, dtype=jnp.int32)
    comp_ids = (record_ids // (N_GX * N_GY * OBS_DEV)).astype(jnp.int32)
    owners = obs_dest[:, 0]
    cell_x = owners // N_GY * CX + obs_col // CY
    cell_y = owners % N_GY * CY + obs_col % CY
    weighted = obs_op * jnp.sqrt(obs_prec)[:, None]
    sampled = second[comp_ids, :, :, cell_x, cell_y].reshape(OBS_ALL, 2 * L)
    innovation = lax.optimization_barrier(jnp.sum(sampled * weighted, axis=1))
    spread = (weighted * innovation[:, None]).reshape(OBS_ALL, 2, L)
    adjoint_obs = jnp.zeros_like(second).at[comp_ids, :, :, cell_x, cell_y].add(spread)
    adjoint_init = pullback(adjoint_obs)[0]
    return background[:, :, :, None, None] * state_incr + adjoint_init
```

```python
import jax
import jax.numpy as jnp
from jax import lax
from jax.experimental import pallas as pl
from jax.experimental.pallas import tpu as pltpu
from jax.sharding import PartitionSpec as P

MESH = pl.DeviceIdType.MESH
F32 = jnp.float32
BF16 = jnp.bfloat16
CHUNKS = 4
GROUP = 32


def coordinates(gx, gy):
    return gy // 4, gx // 2, (gy % 4) * 2 + gx % 2


def device(x, y, z):
    return {"gx": y * 2 + z % 2, "gy": x * 4 + z // 2}


def split(value):
    high = value.astype(BF16)
    return high, (value - high.astype(F32)).astype(BF16)


def matmul(a, b):
    return lax.dot_general(a, b, (((1,), (0,)), ((), ())), preferred_element_type=F32)


def matmul_nt(a, b):
    return lax.dot_general(a, b, (((1,), (1,)), ((), ())), preferred_element_type=F32)


def kernel(
    state_hbm, winds_hbm, op_hbm, meta_ref, gamma_ref, out_hbm,
    cells, spare, winds, ops, send, recv,
    row_out, row_in, lane_out, lane_in, top_out, top_in,
    second_hi, second_lo, select,
    load_sem, op_sem, store_sem, a2a_send, a2a_recv, halo_send, halo_recv, top_send, top_recv, plane_sem, line_sem,
):
    comp = lax.axis_index("comp")
    gx = lax.axis_index("gx")
    gy = lax.axis_index("gy")
    x, y, z = coordinates(gx, gy)
    levels = 128

    load_state = pltpu.make_async_copy(state_hbm, cells, load_sem.at[0])
    load_winds = pltpu.make_async_copy(winds_hbm, winds, load_sem.at[1])
    load_ops = pltpu.make_async_copy(op_hbm, ops, op_sem)
    load_state.start()
    load_ops.start()
    load_winds.start()

    neighbours = (
        {"gx": (gx + 1) % 8},
        {"gx": (gx + 7) % 8},
        {"gy": (gy + 1) % 16},
        {"gy": (gy + 15) % 16},
    )
    partner = {"comp": 1 - comp}

    barrier = pltpu.get_barrier_semaphore()

    def greet(semaphore, target):
        pl.semaphore_signal(semaphore, inc=1, device_id=target, device_id_type=MESH)

    greet(barrier, partner)
    for target in neighbours:
        greet(barrier, target)
    for step in range(1, 4):
        greet(barrier, device((x + step) % 4, y, z))
    for step in range(1, 4):
        greet(barrier, device(x, (y + step) % 4, z))
    for step in range(1, 8):
        greet(barrier, device(x, y, (z + step) % 8))

    row = lax.broadcasted_iota(jnp.int32, (16, 128), 0)
    lane = lax.broadcasted_iota(jnp.int32, (16, 128), 1)
    has_low = jnp.where(gx > 0, 1.0, 0.0)
    has_high = jnp.where(gx < 7, 1.0, 0.0)
    has_left = jnp.where(gy > 0, 1.0, 0.0)
    has_right = jnp.where(gy < 15, 1.0, 0.0)
    gamma = gamma_ref[...]
    own_share = jnp.where(comp == 0, 1.0, 0.5)
    peer_share = 1.5 - own_share

    def halo_copies(sweep):
        pairs = (
            (row_out.at[sweep, 0], row_in.at[sweep, 0]),
            (row_out.at[sweep, 1], row_in.at[sweep, 1]),
            (lane_out.at[sweep, 0], lane_in.at[sweep, 0]),
            (lane_out.at[sweep, 1], lane_in.at[sweep, 1]),
        )
        return [
            pltpu.make_async_remote_copy(
                src, dst, halo_send.at[sweep, n], halo_recv.at[sweep, n],
                device_id=neighbours[n], device_id_type=MESH,
            )
            for n, (src, dst) in enumerate(pairs)
        ]

    def top_copy(sweep):
        return pltpu.make_async_remote_copy(
            top_out.at[sweep], top_in.at[sweep], top_send.at[sweep], top_recv.at[sweep],
            device_id=partner, device_id_type=MESH,
        )

    def keep_edges(sweep, fk, k, up, down, right, left, f, carry):
        row_out[sweep, 0, pl.ds(fk, 1), :] = up[15:16]
        row_out[sweep, 1, pl.ds(fk, 1), :] = down[0:1]
        here = lane == k
        rights = jnp.where(here, jnp.broadcast_to(right[:, 127:128], (16, 128)), carry[2 * f])
        lefts = jnp.where(here, jnp.broadcast_to(left[:, 0:1], (16, 128)), carry[2 * f + 1])
        return carry[: 2 * f] + (rights, lefts) + carry[2 * f + 2 :]

    def store_lanes(sweep, carry):
        for f in range(2):
            lane_out[sweep, 0, 16 * f : 16 * f + 16, :] = carry[2 * f]
            lane_out[sweep, 1, 16 * f : 16 * f + 16, :] = carry[2 * f + 1]

    def halos(sweep, fk, f, k):
        low = row_in[sweep, 0, pl.ds(fk, 1), :] * has_low
        high = row_in[sweep, 1, pl.ds(fk, 1), :] * has_high
        left = pltpu.roll(lane_in[sweep, 0, 16 * f : 16 * f + 16, :], (128 - k) % 128, 1) * has_left
        right = pltpu.roll(lane_in[sweep, 1, 16 * f : 16 * f + 16, :], 127 - k, 1) * has_right
        return low, high, left, right

    blank = jnp.zeros((16, 128), F32)

    load_state.wait()

    def raw_edges(k, carry):
        for f in range(2):
            fk = f * levels + k
            value = cells[fk]
            carry = keep_edges(0, fk, k, value, value, value, value, f, carry)
        return carry

    store_lanes(0, lax.fori_loop(0, levels, raw_edges, (blank,) * 4, unroll=4))
    pl.semaphore_wait(barrier, 18)
    first_halo = halo_copies(0)
    for copy in first_halo:
        copy.start()
    for step in range(1, 4):
        greet(plane_sem, device(x, (y + step) % 4, z))

    load_ops.wait()
    owner = meta_ref[0:1, :].astype(jnp.int32)
    owner_gx, owner_gy = owner // 16, owner % 16
    owner_x, owner_y, owner_z = owner_gy // 4, owner_gx // 2, (owner_gy % 4) * 2 + owner_gx % 2
    relative = ((owner_y - y + 4) % 4) * 32 + ((owner_x - x + 4) % 4) * 8 + (owner_z - z + 8) % 8
    tile_iota = lax.broadcasted_iota(jnp.int32, (128, 512), 0)
    hits = jnp.where(tile_iota == relative, 1.0, 0.0)
    hits_narrow = hits.astype(BF16)
    earlier = jnp.where(
        lax.broadcasted_iota(jnp.int32, (512, 512), 0) < lax.broadcasted_iota(jnp.int32, (512, 512), 1), 1.0, 0.0
    ).astype(BF16)
    slot = jnp.sum(matmul(hits_narrow, earlier) * hits, axis=0, keepdims=True).astype(jnp.int32)
    position = relative * 8 + slot
    column = meta_ref[1:2, :].astype(jnp.int32)
    in_row = tile_iota == (relative % 16) * 8 + slot
    column_high = jnp.where(in_row, (column // 128).astype(F32), 0.0).astype(BF16)
    column_low = jnp.where(in_row, (column % 128).astype(F32), 0.0).astype(BF16)
    columns = 128.0 * matmul_nt(hits_narrow, column_high) + matmul_nt(hits_narrow, column_low)
    send[:, 16, :] = columns
    scale_high, scale_low = split(jnp.broadcast_to(jnp.sqrt(meta_ref[2:3, :]), (128, 512)))
    ops_high, ops_low = split(ops[...])

    def pack(chunk, _):
        slots = lax.broadcasted_iota(jnp.int32, (256, 512), 0) + chunk * 256
        pick = jnp.where(slots == position, 1.0, 0.0).astype(BF16)
        scale = matmul_nt(pick, scale_high) + matmul_nt(pick, scale_low)
        rows = matmul(pick, ops_high) + matmul(pick, ops_low)
        target = pl.ds(chunk * GROUP, GROUP)
        send[target, 0:8, :] = (rows[:, :128] * scale).reshape(GROUP, 8, 128)
        send[target, 8:16, :] = (rows[:, 128:] * scale).reshape(GROUP, 8, 128)
        return 0

    lax.fori_loop(0, CHUNKS, pack, 0)
    pl.semaphore_wait(plane_sem, 3)
    for step in range(1, 8):
        greet(line_sem, device(x, y, (z + step) % 8))
    pl.semaphore_wait(line_sem, 7)

    pltpu.make_async_copy(send.at[0], recv.at[0], a2a_recv.at[0]).start()

    def dispatch(s, _):
        target = device((x + (s // 8) % 4) % 4, (y + s // 32) % 4, (z + s % 8) % 8)
        pltpu.make_async_remote_copy(
            send.at[s], recv.at[s], a2a_send, a2a_recv.at[s // GROUP],
            device_id=target, device_id_type=MESH,
        ).start()
        return 0

    lax.fori_loop(1, 128, dispatch, 0)

    load_winds.wait()

    def forward(sweep, source, target, last):
        def level(k, carry):
            wind_x = winds[k]
            wind_y = winds[levels + k]
            for f in range(2):
                fk = f * levels + k
                here = source[fk]
                above = source[f * levels + jnp.minimum(k + 1, levels - 1)]
                below = source[f * levels + jnp.maximum(k - 1, 0)]
                low, high, left, right = halos(sweep, fk, f, k)
                up = jnp.where(row == 15, high, pltpu.roll(here, 15, 0))
                down = jnp.where(row == 0, low, pltpu.roll(here, 1, 0))
                east = jnp.where(lane == 127, right, pltpu.roll(here, 127, 1))
                west = jnp.where(lane == 0, left, pltpu.roll(here, 1, 1))
                value = (
                    0.3 * here + 0.15 * (above + below) + 0.1 * ((up + down) + (east + west))
                    - 0.5 * (wind_x * (up - down) + wind_y * (east - west))
                )
                target[fk] = value
                if not last:
                    carry = keep_edges(sweep + 1, fk, k, value, value, value, value, f, carry)
            return carry

        level(0, (blank,) * 4)
        for f in range(2):
            top_out[sweep, 16 * f : 16 * f + 16, :] = target[f * levels]
        copy = top_copy(sweep)
        copy.start()
        carry = lax.fori_loop(1, levels, level, (blank,) * 4, unroll=4)
        copy.wait_recv()
        for f in range(2):
            own = target[f * levels]
            value = own - own_share * gamma * (own - top_in[sweep, 16 * f : 16 * f + 16, :])
            target[f * levels] = value
            if not last:
                carry = keep_edges(sweep + 1, f * levels, 0, value, value, value, value, f, carry)
        if not last:
            store_lanes(sweep + 1, carry)
        return copy

    for copy in first_halo:
        copy.wait_recv()
    first_top = forward(0, cells, spare, False)
    second_halo = halo_copies(1)
    for copy in second_halo:
        copy.start()
    for copy in second_halo:
        copy.wait_recv()
    second_top = forward(1, spare, cells, True)

    flat_cells = cells.reshape(256 * 16, 128)
    for i in range(16):
        high, low = split(flat_cells[pl.ds(i, 256, stride=16), :])
        second_hi[:, 128 * i : 128 * i + 128] = high
        second_lo[:, 128 * i : 128 * i + 128] = low

    def clear(fk, _):
        spare[fk] = blank
        return 0

    lax.fori_loop(0, 256, clear, 0, unroll=8)
    flat_spare = spare.reshape(256 * 16, 128)

    def observe(chunk, _):
        arrived = recv.at[pl.ds(chunk * GROUP, GROUP)]
        pltpu.make_async_copy(arrived, arrived, a2a_recv.at[chunk]).wait()
        first = pl.ds(chunk * GROUP, 16)
        other = pl.ds(chunk * GROUP + 16, 16)
        where = jnp.concatenate(
            [jnp.sum(recv[first, 16, :], axis=0, keepdims=True), jnp.sum(recv[other, 16, :], axis=0, keepdims=True)],
            axis=1,
        ).astype(jnp.int32)
        for part in range(8):
            cell = lax.broadcasted_iota(jnp.int32, (256, 256), 0) + 256 * part
            select[256 * part : 256 * part + 256, :] = jnp.where(cell == where, 1.0, 0.0).astype(BF16)
        group = pl.ds(chunk * GROUP, GROUP)
        weights = jnp.concatenate(
            [recv[group, 0:8, :].reshape(256, 128).T, recv[group, 8:16, :].reshape(256, 128).T], axis=0
        )
        sampled = matmul(second_hi[...], select[...]) + matmul(second_lo[...], select[...])
        innovation = jnp.sum(sampled * weights, axis=0, keepdims=True)
        spread_high, spread_low = split(weights * innovation)
        for i in range(16):
            cells_of_row = select[128 * i : 128 * i + 128, :]
            flat_spare[pl.ds(i, 256, stride=16), :] += matmul_nt(spread_high, cells_of_row) + matmul_nt(
                spread_low, cells_of_row
            )
        return 0

    lax.fori_loop(0, CHUNKS, observe, 0)

    def adjoint(sweep, source, target, last):
        for f in range(2):
            top_out[sweep, 16 * f : 16 * f + 16, :] = source[f * levels]
        top = top_copy(sweep)
        top.start()

        def parts(fk, k):
            here = source[fk]
            even = 0.1 * here
            along_x = 0.5 * winds[k] * here
            along_y = 0.5 * winds[levels + k] * here
            return here, even - along_x, even + along_x, even - along_y, even + along_y

        def edges(k, carry):
            for f in range(2):
                fk = f * levels + k
                _, up, down, right, left = parts(fk, k)
                carry = keep_edges(sweep, fk, k, up, down, right, left, f, carry)
            return carry

        carry = lax.fori_loop(1, levels, edges, (blank,) * 4, unroll=4)
        top.wait_recv()
        for f in range(2):
            own = source[f * levels]
            source[f * levels] = (
                own - own_share * gamma * own + peer_share * gamma * top_in[sweep, 16 * f : 16 * f + 16, :]
            )
        store_lanes(sweep, edges(0, carry))
        copies = halo_copies(sweep)
        for copy in copies:
            copy.start()

        def inside(k, _):
            for f in range(2):
                fk = f * levels + k
                here, up, down, right, left = parts(fk, k)
                above = source[f * levels + jnp.minimum(k + 1, levels - 1)]
                below = source[f * levels + jnp.maximum(k - 1, 0)]
                target[fk] = (
                    0.3 * here + 0.15 * (above + below)
                    + jnp.where(row == 0, 0.0, pltpu.roll(up, 1, 0))
                    + jnp.where(row == 15, 0.0, pltpu.roll(down, 15, 0))
                    + jnp.where(lane == 0, 0.0, pltpu.roll(right, 1, 1))
                    + jnp.where(lane == 127, 0.0, pltpu.roll(left, 127, 1))
                )
            return 0

        lax.fori_loop(0, levels, inside, 0, unroll=4)
        for copy in copies:
            copy.wait_recv()

        def outside(k, _):
            for f in range(2):
                fk = f * levels + k
                low, high, left, right = halos(sweep, fk, f, k)
                target[fk] = (
                    target[fk]
                    + jnp.where(row == 0, low, 0.0) + jnp.where(row == 15, high, 0.0)
                    + jnp.where(lane == 0, left, 0.0) + jnp.where(lane == 127, right, 0.0)
                )
            return 0

        lax.fori_loop(0, levels, outside, 0, unroll=4)
        return [top] + copies

    started = [first_top, second_top] + first_halo + second_halo
    started += adjoint(2, spare, cells, False)
    started += adjoint(3, cells, spare, True)
    store = pltpu.make_async_copy(spare, out_hbm, store_sem)
    store.start()
    for copy in started:
        copy.wait_send()
    sent = recv.at[pl.ds(1, 127)]
    pltpu.make_async_copy(sent, sent, a2a_send).wait()
    store.wait()


def local(state_incr, winds, coupling, background, obs_dest, obs_col, obs_op, obs_prec):
    shape = state_incr.shape[1:]
    slabs = shape[0] * shape[1]
    meta = jnp.stack([obs_dest[:, 0].astype(F32), obs_col.astype(F32), obs_prec])
    hbm = pl.BlockSpec(memory_space=pl.ANY)
    vmem = pl.BlockSpec(memory_space=pltpu.VMEM)
    tile = (slabs,) + shape[2:]
    adjoint = pl.pallas_call(
        kernel,
        out_shape=jax.ShapeDtypeStruct(tile, F32),
        in_specs=[hbm, hbm, hbm, vmem, vmem],
        out_specs=hbm,
        scratch_shapes=[
            pltpu.VMEM(tile, F32),
            pltpu.VMEM(tile, F32),
            pltpu.VMEM(tile, F32),
            pltpu.VMEM((512, 256), F32),
            pltpu.VMEM((128, 17, 128), F32),
            pltpu.VMEM((128, 17, 128), F32),
            pltpu.VMEM((4, 2, 256, 128), F32),
            pltpu.VMEM((4, 2, 256, 128), F32),
            pltpu.VMEM((4, 2, 32, 128), F32),
            pltpu.VMEM((4, 2, 32, 128), F32),
            pltpu.VMEM((4, 32, 128), F32),
            pltpu.VMEM((4, 32, 128), F32),
            pltpu.VMEM((256, 2048), BF16),
            pltpu.VMEM((256, 2048), BF16),
            pltpu.VMEM((2048, 256), BF16),
            pltpu.SemaphoreType.DMA((2,)),
            pltpu.SemaphoreType.DMA,
            pltpu.SemaphoreType.DMA,
            pltpu.SemaphoreType.DMA,
            pltpu.SemaphoreType.DMA((CHUNKS,)),
            pltpu.SemaphoreType.DMA((4, 4)),
            pltpu.SemaphoreType.DMA((4, 4)),
            pltpu.SemaphoreType.DMA((4,)),
            pltpu.SemaphoreType.DMA((4,)),
            pltpu.SemaphoreType.REGULAR,
            pltpu.SemaphoreType.REGULAR,
        ],
        compiler_params=pltpu.CompilerParams(
            collective_id=0, has_side_effects=True, vmem_limit_bytes=56 * 1024 * 1024
        ),
    )(state_incr.reshape(tile), winds.reshape(tile), obs_op, meta, coupling)
    result = background[0][:, :, None, None] * state_incr[0] + adjoint.reshape(shape)
    return result[None]


def solution(mesh):
    placed = (
        P("comp", None, None, "gx", "gy"),
        P("comp", None, None, "gx", "gy"),
        P("gx", "gy"),
        P("comp", None, None),
        P(("comp", "gx", "gy"), None),
        P(("comp", "gx", "gy")),
        P(("comp", "gx", "gy"), None),
        P(("comp", "gx", "gy")),
    )
    return jax.shard_map(
        local,
        mesh=mesh,
        in_specs=placed,
        out_specs=P("comp", None, None, "gx", "gy"),
        check_vma=False,
    )
```

```python
import jax
import jax.numpy as jnp
from jax import lax
from jax.experimental import pallas as pl
from jax.experimental.pallas import tpu as pltpu
from jax.sharding import PartitionSpec as P

MESH = pl.DeviceIdType.MESH
F32 = jnp.float32
BF16 = jnp.bfloat16
CHUNKS = 4
GROUP = 32
PAD = 144
BLOCK = 32


def device(x, y, z):
    return {"gx": y * 2 + (z & 1), "gy": x * 4 + (z >> 1)}


def split(value):
    high = value.astype(BF16)
    return high, (value - high.astype(F32)).astype(BF16)


def matmul(a, b):
    return lax.dot_general(a, b, (((1,), (0,)), ((), ())), preferred_element_type=F32)


def matmul_nt(a, b):
    return lax.dot_general(a, b, (((1,), (1,)), ((), ())), preferred_element_type=F32)


def kernel(
    state_hbm, winds_hbm, op_hbm, owner_hbm, column_hbm, prec_hbm, gamma_hbm, out_hbm,
    owner_ref, column_ref, prec_ref, gamma_ref, native, native_winds, field_0, field_1, field_2, field_3, wind_x, wind_y, exchange, ops, send, recv,
    row_out, lane_out, lane_in, top_out, top_in,
    second, pick_cell,
    load_sem, store_sem, a2a_send, a2a_recv, halo_send, halo_recv, top_send, top_recv, line_sem,
):
    comp = lax.axis_index("comp")
    gx = lax.axis_index("gx")
    gy = lax.axis_index("gy")
    x, y, z = gy >> 2, gx >> 1, ((gy & 3) << 1) | (gx & 1)

    loads = [
        pltpu.make_async_copy(src, dst, load_sem.at[n])
        for n, (src, dst) in enumerate(
            (
                (owner_hbm, owner_ref), (column_hbm, column_ref), (prec_hbm, prec_ref), (op_hbm, ops),
                (state_hbm, native), (winds_hbm, native_winds), (gamma_hbm, gamma_ref),
            )
        )
    ]
    for load in loads:
        load.start()

    neighbours = (
        {"gx": (gx + 1) & 7},
        {"gx": (gx + 7) & 7},
        {"gy": (gy + 1) & 15},
        {"gy": (gy + 15) & 15},
    )
    partner = {"comp": 1 - comp}
    barrier = pltpu.get_barrier_semaphore()

    def greet(semaphore, target):
        pl.semaphore_signal(semaphore, inc=1, device_id=target, device_id_type=MESH)

    for target in neighbours:
        greet(barrier, target)
    greet(barrier, partner)
    for step in range(1, 8):
        greet(barrier, device(x, y, (z + step) & 7))
    for step in range(1, 16):
        greet(barrier, device((x + step) & 3, (y + step // 4) & 3, z))

    lane = lax.broadcasted_iota(jnp.int32, (BLOCK, 128), 1)
    lane_8 = lax.broadcasted_iota(jnp.int32, (8, 128), 1)
    has_left = jnp.where(gy > 0, 1.0, 0.0)
    has_right = jnp.where(gy < 15, 1.0, 0.0)
    own_share = jnp.where(comp == 0, 1.0, 0.5)
    peer_share = 1.5 - own_share
    fields = (field_0, field_1, field_2, field_3)
    flat_fields = [field.reshape(2 * 18 * PAD, 128) for field in fields]
    flat_native = native.reshape(4096, 128)
    flat_winds = native_winds.reshape(4096, 128)
    flat_wind_y = wind_y.reshape(16 * PAD, 128)

    def edge_row(f, j):
        return pl.ds((f * 18 + 1) * PAD + 8 + j, 16, stride=PAD)

    def halo_copies(sweep, sources):
        pairs = (
            (sources[0], fields[sweep].at[:, 0, pl.ds(8, 128), :]),
            (sources[1], fields[sweep].at[:, 17, pl.ds(8, 128), :]),
            (lane_out.at[sweep, 0], lane_in.at[sweep, 0]),
            (lane_out.at[sweep, 1], lane_in.at[sweep, 1]),
        )
        return [
            pltpu.make_async_remote_copy(
                src, dst, halo_send.at[sweep, n], halo_recv.at[sweep, n],
                device_id=neighbours[n], device_id_type=MESH,
            )
            for n, (src, dst) in enumerate(pairs)
        ]

    def start_tangent_halo(sweep):
        copies = halo_copies(
            sweep, (fields[sweep].at[:, 16, pl.ds(8, 128), :], fields[sweep].at[:, 1, pl.ds(8, 128), :])
        )
        copies[0].start()
        copies[1].start()
        for f in range(2):
            lane_out[sweep, 0, 16 * f : 16 * f + 16, :] = flat_fields[sweep][edge_row(f, 127), :]
            lane_out[sweep, 1, 16 * f : 16 * f + 16, :] = flat_fields[sweep][edge_row(f, 0), :]
        copies[2].start()
        copies[3].start()
        return copies

    def take_lanes(sweep, copies):
        copies[2].wait_recv()
        copies[3].wait_recv()
        for f in range(2):
            flat_fields[sweep][edge_row(f, -1), :] = lane_in[sweep, 0, 16 * f : 16 * f + 16, :] * has_left
            flat_fields[sweep][edge_row(f, 128), :] = lane_in[sweep, 1, 16 * f : 16 * f + 16, :] * has_right

    def take_rows(sweep, copies):
        copies[0].wait_recv()
        copies[1].wait_recv()

        @pl.when(gx == 0)
        def _():
            fields[sweep][:, 0, 8:136, :] = jnp.zeros((2, 128, 128), F32)

        @pl.when(gx == 7)
        def _():
            fields[sweep][:, 17, 8:136, :] = jnp.zeros((2, 128, 128), F32)

    def pack_top(sweep, part, field, i):
        for f in range(2):
            rows = pl.ds(f * 16 + (i >> 3) * 8, 8)
            packed = top_out[sweep, part, rows, :]
            base = (i & 7) * 16
            for n in range(16):
                level = fields[field][f, i + 1, 8 + 8 * n : 16 + 8 * n, 0:1]
                packed = jnp.where(lane_8 == base + n, jnp.broadcast_to(level, (8, 128)), packed)
            top_out[sweep, part, rows, :] = packed

    def top_copy(sweep, part):
        return pltpu.make_async_remote_copy(
            top_out.at[sweep, part], top_in.at[sweep, part], top_send.at[sweep, part], top_recv.at[sweep, part],
            device_id=partner, device_id_type=MESH,
        )

    def couple(sweep, part, field, i, transposed):
        for f in range(2):
            rows = pl.ds(f * 16 + (i >> 3) * 8, 8)
            packed = pltpu.roll(top_in[sweep, part, rows, :], (128 - (i & 7) * 16) & 127, 1)
            for half in range(2):
                low = 8 + 64 * half
                own = fields[field][f, i + 1, low : low + 64, :]
                peer = jnp.concatenate(
                    [packed if n == 0 else pltpu.roll(packed, 128 - n, 1) for n in range(8 * half, 8 * half + 8)], axis=0
                )
                rate = exchange[i, 64 * half : 64 * half + 64, :]
                if transposed:
                    value = own - rate * (own_share * own - peer_share * peer)
                else:
                    value = own - rate * (own_share * (own - peer))
                fields[field][f, i + 1, low : low + 64, :] = value

    def vertical(here):
        above = jnp.where(lane == 127, here, pltpu.roll(here, 127, 1))
        below = jnp.where(lane == 0, here, pltpu.roll(here, 1, 1))
        return 0.3 * here + 0.15 * (above + below)

    def neighbourhood(field, f, i, low):
        here = field[f, i + 1, low : low + BLOCK, :]
        up = field[f, i + 2, low : low + BLOCK, :]
        down = field[f, i, low : low + BLOCK, :]
        right = field[f, i + 1, low + 1 : low + 1 + BLOCK, :]
        left = field[f, i + 1, low - 1 : low - 1 + BLOCK, :]
        return here, up, down, right, left

    def tangent_row(sweep, target, i):
        for block in range(128 // BLOCK):
            low = 8 + block * BLOCK
            u = wind_x[i + 1, block * BLOCK : (block + 1) * BLOCK, :]
            w = wind_y[i, low : low + BLOCK, :]
            for f in range(2):
                here, up, down, right, left = neighbourhood(fields[sweep], f, i, low)
                fields[target][f, i + 1, low : low + BLOCK, :] = (
                    vertical(here) + 0.1 * ((up + down) + (right + left)) - (u * (up - down) + w * (right - left))
                )

    def adjoint_row(sweep, target, i):
        for block in range(128 // BLOCK):
            low = 8 + block * BLOCK
            inner = slice(block * BLOCK, (block + 1) * BLOCK)
            from_down = 0.1 - wind_x[i, inner, :]
            from_up = 0.1 + wind_x[i + 2, inner, :]
            from_left = 0.1 - wind_y[i, low - 1 : low - 1 + BLOCK, :]
            from_right = 0.1 + wind_y[i, low + 1 : low + 1 + BLOCK, :]
            for f in range(2):
                here, up, down, right, left = neighbourhood(fields[sweep], f, i, low)
                fields[target][f, i + 1, low : low + BLOCK, :] = (
                    vertical(here) + (from_down * down + from_up * up) + (from_left * left + from_right * right)
                )

    def each(body, low=0, high=16):
        def step(i, _):
            body(i)
            return 0

        lax.fori_loop(low, high, step, 0)

    for load in loads[:4]:
        load.wait()
    owner = owner_ref[...]
    owner_gx, owner_gy = owner >> 4, owner & 15
    owner_x, owner_y, owner_z = owner_gy >> 2, owner_gx >> 1, ((owner_gy & 3) << 1) | (owner_gx & 1)
    relative = ((owner_y - y + 4) & 3) * 32 + ((owner_x - x + 4) & 3) * 8 + ((owner_z - z + 8) & 7)
    tile_iota = lax.broadcasted_iota(jnp.int32, (128, 512), 0)
    hits = jnp.where(tile_iota == relative, 1.0, 0.0)
    hits_narrow = hits.astype(BF16)
    earlier = jnp.where(
        lax.broadcasted_iota(jnp.int32, (512, 512), 0) < lax.broadcasted_iota(jnp.int32, (512, 512), 1), 1.0, 0.0
    ).astype(BF16)
    slot = jnp.sum(matmul(hits_narrow, earlier) * hits, axis=0, keepdims=True).astype(jnp.int32)
    position = relative * 8 + slot
    column = column_ref[...]
    in_row = tile_iota == (relative & 15) * 8 + slot
    column_high = jnp.where(in_row, (column >> 7).astype(F32), 0.0).astype(BF16)
    column_low = jnp.where(in_row, (column & 127).astype(F32), 0.0).astype(BF16)
    send[:, 16, :] = 128.0 * matmul_nt(hits_narrow, column_high) + matmul_nt(hits_narrow, column_low)
    scale_high, scale_low = split(jnp.broadcast_to(jnp.sqrt(prec_ref[...]), (128, 512)))
    ops_high, ops_low = split(ops[...])

    def pack(chunk, _):
        slots = lax.broadcasted_iota(jnp.int32, (256, 512), 0) + chunk * 256
        pick = jnp.where(slots == position, 1.0, 0.0).astype(BF16)
        scale = matmul_nt(pick, scale_high) + matmul_nt(pick, scale_low)
        rows = matmul(pick, ops_high) + matmul(pick, ops_low)
        target = pl.ds(chunk * GROUP, GROUP)
        send[target, 0:8, :] = (rows[:, :128] * scale).reshape(GROUP, 8, 128)
        send[target, 8:16, :] = (rows[:, 128:] * scale).reshape(GROUP, 8, 128)
        return 0

    lax.fori_loop(0, CHUNKS, pack, 0)

    top_out[...] = jnp.zeros((4, 2, 32, 128), F32)

    loads[4].wait()

    def turn_state(i):
        for f in range(2):
            field_0[f, i + 1, 8:136, :] = flat_native[pl.ds(f * 2048 + i, 128, stride=16), :].T

    each(turn_state)
    pl.semaphore_wait(barrier, 27)
    for step in range(1, 8):
        greet(line_sem, device(x, y, (z + step) & 7))
    first_halo = start_tangent_halo(0)
    pl.semaphore_wait(line_sem, 7)

    pltpu.make_async_copy(send.at[0], recv.at[0], a2a_recv.at[0]).start()

    def dispatch(s, _):
        target = device((x + ((s >> 3) & 3)) & 3, (y + (s >> 5)) & 3, (z + (s & 7)) & 7)
        pltpu.make_async_remote_copy(
            send.at[s], recv.at[s], a2a_send, a2a_recv.at[s >> 5], device_id=target, device_id_type=MESH,
        ).start()
        return 0

    lax.fori_loop(1, 64, dispatch, 0)

    loads[5].wait()
    loads[6].wait()
    wind_x[0] = jnp.full((128, 128), -0.9, F32)
    wind_x[17] = jnp.full((128, 128), 0.9, F32)

    def turn_winds(i):
        wind_x[i + 1] = 0.5 * flat_winds[pl.ds(i, 128, stride=16), :].T
        wind_y[i, 8:136, :] = 0.5 * flat_winds[pl.ds(2048 + i, 128, stride=16), :].T
        wind_y[i, 0:8, :] = jnp.full((8, 128), -0.9, F32)
        wind_y[i, 136:144, :] = jnp.full((8, 128), 0.9, F32)
        rate = jnp.broadcast_to(gamma_ref[pl.ds(i, 1), :], (128, 128)).T
        exchange[i] = jnp.where(lax.broadcasted_iota(jnp.int32, (128, 128), 1) == 0, rate, 0.0)

    each(turn_winds)

    tops = []

    def sweep_rows(sweep, copies, compute, target, meet, after):
        take_lanes(sweep, copies)

        def inside(i):
            compute(i)
            if meet is not None:
                pack_top(meet, 0, target, i)

        each(inside, 1, 15)
        if meet is not None:
            inner = top_copy(meet, 0)
            inner.start()
            tops.append(inner)
            inner.wait_recv()
        each(lambda i: after(i, 0), 1, 15)
        take_rows(sweep, copies)
        for i in (0, 15):
            compute(i)
            if meet is not None:
                pack_top(meet, 1, target, i)
        if meet is not None:
            outer = top_copy(meet, 1)
            outer.start()
            tops.append(outer)
            outer.wait_recv()
        for i in (0, 15):
            after(i, 1)

    sweep_rows(
        0, first_halo, lambda i: tangent_row(0, 1, i), 1, 0, lambda i, part: couple(0, part, 1, i, False)
    )
    second_halo = start_tangent_halo(1)
    lax.fori_loop(64, 128, dispatch, 0)

    def finish_second(i, part):
        couple(1, part, 2, i, False)
        for f in range(2):
            high, low = split(field_2[f, i + 1, 8:136, :])
            second[pl.ds(i * 128, 128), 128 * f : 128 * f + 128] = high
            second[pl.ds(i * 128, 128), 256 + 128 * f : 384 + 128 * f] = low
            field_2[f, i + 1, 8:136, :] = jnp.zeros((128, 128), F32)

    sweep_rows(1, second_halo, lambda i: tangent_row(1, 2, i), 2, 1, finish_second)
    for copy in second_halo:
        copy.wait_send()

    def observe(chunk, _):
        arrived = recv.at[pl.ds(chunk * GROUP, GROUP)]
        pltpu.make_async_copy(arrived, arrived, a2a_recv.at[chunk]).wait()
        group = pl.ds(chunk * GROUP, GROUP)
        where = jnp.concatenate(
            [
                jnp.sum(recv[pl.ds(chunk * GROUP, 16), 16, :], axis=0, keepdims=True),
                jnp.sum(recv[pl.ds(chunk * GROUP + 16, 16), 16, :], axis=0, keepdims=True),
            ],
            axis=1,
        ).astype(jnp.int32)
        down_rows = jnp.broadcast_to(where, (128, 256)).T
        within = lax.broadcasted_iota(jnp.int32, (256, 128), 1)
        for i in range(16):
            pick_cell[:, 128 * i : 128 * i + 128] = jnp.where(down_rows == within + 128 * i, 1.0, 0.0).astype(BF16)
        both = matmul(pick_cell[...], second[...])
        sampled = both[:, :256] + both[:, 256:]
        weights = jnp.concatenate(
            [recv[group, 0:8, :].reshape(256, 128), recv[group, 8:16, :].reshape(256, 128)], axis=1
        )
        spread = jnp.concatenate(split(weights * jnp.sum(sampled * weights, axis=1, keepdims=True)), axis=0)

        def scatter(quarter):
            cell = lax.broadcasted_iota(jnp.int32, (512, 256), 0) + quarter * 512
            pick = jnp.where(cell == where, 1.0, 0.0).astype(BF16)
            added = matmul(jnp.concatenate([pick, pick], axis=1), spread)
            for r in range(4):
                for f in range(2):
                    field_2[f, quarter * 4 + r + 1, 8:136, :] += added[
                        128 * r : 128 * r + 128, 128 * f : 128 * f + 128
                    ]

        each(scatter, 0, 4)
        return 0

    lax.fori_loop(0, CHUNKS, observe, 0)

    def start_adjoint_halo(sweep):
        copies = halo_copies(sweep, (row_out.at[sweep - 2, 0], row_out.at[sweep - 2, 1]))
        for f in range(2):
            row_out[sweep - 2, 0, f] = (0.1 - wind_x[16]) * fields[sweep][f, 16, 8:136, :]
            row_out[sweep - 2, 1, f] = (0.1 + wind_x[1]) * fields[sweep][f, 1, 8:136, :]
        copies[0].start()
        copies[1].start()
        return copies

    def start_adjoint_lanes(sweep, copies):
        right = 0.1 - flat_wind_y[pl.ds(8 + 127, 16, stride=PAD), :]
        left = 0.1 + flat_wind_y[pl.ds(8, 16, stride=PAD), :]
        for f in range(2):
            lane_out[sweep, 0, 16 * f : 16 * f + 16, :] = right * flat_fields[sweep][edge_row(f, 127), :]
            lane_out[sweep, 1, 16 * f : 16 * f + 16, :] = left * flat_fields[sweep][edge_row(f, 0), :]
        copies[2].start()
        copies[3].start()

    for i in (0, 15):
        pack_top(2, 1, 2, i)
    outer_top = top_copy(2, 1)
    outer_top.start()
    each(lambda i: pack_top(2, 0, 2, i), 1, 15)
    inner_top = top_copy(2, 0)
    inner_top.start()
    outer_top.wait_recv()
    for i in (0, 15):
        couple(2, 1, 2, i, True)
    third_halo = start_adjoint_halo(2)
    inner_top.wait_recv()
    each(lambda i: couple(2, 0, 2, i, True), 1, 15)
    start_adjoint_lanes(2, third_halo)
    sweep_rows(2, third_halo, lambda i: adjoint_row(2, 3, i), 3, 3, lambda i, part: couple(3, part, 3, i, True))
    fourth_halo = start_adjoint_halo(3)
    start_adjoint_lanes(3, fourth_halo)

    def turn_back(i, part):
        for f in range(2):
            flat_native[pl.ds(f * 2048 + i, 128, stride=16), :] = field_1[f, i + 1, 8:136, :].T

    sweep_rows(3, fourth_halo, lambda i: adjoint_row(3, 1, i), 1, None, turn_back)
    started = tops + [outer_top, inner_top] + first_halo + third_halo + fourth_halo
    store = pltpu.make_async_copy(native, out_hbm, store_sem)
    store.start()
    for copy in started:
        copy.wait_send()
    sent = recv.at[pl.ds(1, 127)]
    pltpu.make_async_copy(sent, sent, a2a_send).wait()
    store.wait()


def local(state_incr, winds, coupling, background, obs_dest, obs_col, obs_op, obs_prec):
    shape = state_incr.shape[1:]
    tile = (shape[0] * shape[1],) + shape[2:]
    hbm = pl.BlockSpec(memory_space=pltpu.HBM)
    adjoint = pl.pallas_call(
        kernel,
        out_shape=jax.ShapeDtypeStruct(tile, F32),
        in_specs=[hbm] * 7,
        out_specs=pl.BlockSpec(memory_space=pl.ANY),
        scratch_shapes=[
            pltpu.VMEM((1, 512), jnp.int32),
            pltpu.VMEM((1, 512), jnp.int32),
            pltpu.VMEM((1, 512), F32),
            pltpu.VMEM((16, 128), F32),
            pltpu.VMEM(tile, F32),
            pltpu.VMEM(tile, F32),
            pltpu.VMEM((2, 18, PAD, 128), F32),
            pltpu.VMEM((2, 18, PAD, 128), F32),
            pltpu.VMEM((2, 18, PAD, 128), F32),
            pltpu.VMEM((2, 18, PAD, 128), F32),
            pltpu.VMEM((18, 128, 128), F32),
            pltpu.VMEM((16, PAD, 128), F32),
            pltpu.VMEM((16, 128, 128), F32),
            pltpu.VMEM((512, 256), F32),
            pltpu.VMEM((128, 17, 128), F32),
            pltpu.VMEM((128, 17, 128), F32),
            pltpu.VMEM((2, 2, 2, 128, 128), F32),
            pltpu.VMEM((4, 2, 32, 128), F32),
            pltpu.VMEM((4, 2, 32, 128), F32),
            pltpu.VMEM((4, 2, 32, 128), F32),
            pltpu.VMEM((4, 2, 32, 128), F32),
            pltpu.VMEM((2048, 512), BF16),
            pltpu.VMEM((256, 2048), BF16),
            pltpu.SemaphoreType.DMA((7,)),
            pltpu.SemaphoreType.DMA,
            pltpu.SemaphoreType.DMA,
            pltpu.SemaphoreType.DMA((CHUNKS,)),
            pltpu.SemaphoreType.DMA((4, 4)),
            pltpu.SemaphoreType.DMA((4, 4)),
            pltpu.SemaphoreType.DMA((4, 2)),
            pltpu.SemaphoreType.DMA((4, 2)),
            pltpu.SemaphoreType.REGULAR,
        ],
        compiler_params=pltpu.CompilerParams(
            collective_id=0, has_side_effects=True, vmem_limit_bytes=60 * 1024 * 1024
        ),
    )(
        state_incr.reshape(tile), winds.reshape(tile), obs_op,
        obs_dest.reshape(1, -1), obs_col.reshape(1, -1), obs_prec.reshape(1, -1), coupling,
    )
    result = background[0][:, :, None, None] * state_incr[0] + adjoint.reshape(shape)
    return result[None]


def solution(mesh):
    placed = (
        P("comp", None, None, "gx", "gy"),
        P("comp", None, None, "gx", "gy"),
        P("gx", "gy"),
        P("comp", None, None),
        P(("comp", "gx", "gy"), None),
        P(("comp", "gx", "gy")),
        P(("comp", "gx", "gy"), None),
        P(("comp", "gx", "gy")),
    )
    return jax.shard_map(
        local,
        mesh=mesh,
        in_specs=placed,
        out_specs=P("comp", None, None, "gx", "gy"),
        check_vma=False,
    )
```

```python
import jax
import jax.numpy as jnp
from jax import lax
from jax.experimental import pallas as pl
from jax.experimental.pallas import tpu as pltpu
from jax.sharding import PartitionSpec as P

MESH = pl.DeviceIdType.MESH
F32 = jnp.float32
BF16 = jnp.bfloat16
CHUNKS = 4
GROUP = 32
PAD = 144
BLOCK = 32


def device(x, y, z):
    return {"gx": y * 2 + (z & 1), "gy": x * 4 + (z >> 1)}


def split(value):
    high = value.astype(BF16)
    return high, (value - high.astype(F32)).astype(BF16)


def matmul(a, b):
    return lax.dot_general(a, b, (((1,), (0,)), ((), ())), preferred_element_type=F32)


def matmul_nt(a, b):
    return lax.dot_general(a, b, (((1,), (1,)), ((), ())), preferred_element_type=F32)


def kernel(
    state_hbm, winds_hbm, op_hbm, owner_hbm, column_hbm, prec_hbm, gamma_hbm, out_hbm,
    owner_ref, column_ref, prec_ref, gamma_ref, native, native_winds, field_0, field_1, field_2, field_3, wind_x, wind_y, exchange, ops, send, recv,
    row_out, lane_out, lane_in, top_out, top_in,
    second, pick_cell,
    load_sem, store_sem, a2a_send, a2a_recv, halo_send, halo_recv, top_send, top_recv, line_sem,
):
    comp = lax.axis_index("comp")
    gx = lax.axis_index("gx")
    gy = lax.axis_index("gy")
    x, y, z = gy >> 2, gx >> 1, ((gy & 3) << 1) | (gx & 1)

    loads = [
        pltpu.make_async_copy(src, dst, load_sem.at[n])
        for n, (src, dst) in enumerate(
            (
                (owner_hbm, owner_ref), (column_hbm, column_ref), (prec_hbm, prec_ref), (op_hbm, ops),
                (state_hbm, native), (winds_hbm, native_winds), (gamma_hbm, gamma_ref),
            )
        )
    ]
    for load in loads:
        load.start()

    neighbours = (
        {"gx": (gx + 1) & 7},
        {"gx": (gx + 7) & 7},
        {"gy": (gy + 1) & 15},
        {"gy": (gy + 15) & 15},
    )
    partner = {"comp": 1 - comp}
    barrier = pltpu.get_barrier_semaphore()

    def greet(semaphore, target):
        pl.semaphore_signal(semaphore, inc=1, device_id=target, device_id_type=MESH)

    for target in neighbours:
        greet(barrier, target)
    greet(barrier, partner)
    for step in range(1, 8):
        greet(barrier, device(x, y, (z + step) & 7))
    for step in range(1, 16):
        greet(barrier, device((x + step) & 3, (y + step // 4) & 3, z))

    lane = lax.broadcasted_iota(jnp.int32, (BLOCK, 128), 1)
    lane_8 = lax.broadcasted_iota(jnp.int32, (8, 128), 1)
    has_left = jnp.where(gy > 0, 1.0, 0.0)
    has_right = jnp.where(gy < 15, 1.0, 0.0)
    own_share = jnp.where(comp == 0, 1.0, 0.5)
    peer_share = 1.5 - own_share
    fields = (field_0, field_1, field_2, field_3)
    flat_fields = [field.reshape(2 * 18 * PAD, 128) for field in fields]
    flat_native = native.reshape(4096, 128)
    flat_winds = native_winds.reshape(4096, 128)
    flat_wind_y = wind_y.reshape(16 * PAD, 128)

    def edge_row(f, j, first=0, count=16):
        return pl.ds((f * 18 + 1 + first) * PAD + 8 + j, count, stride=PAD)

    def halo_copies(sweep, sources):
        pairs = (
            (sources[0], fields[sweep].at[:, 0, pl.ds(8, 128), :]),
            (sources[1], fields[sweep].at[:, 17, pl.ds(8, 128), :]),
            (lane_out.at[sweep, 0], lane_in.at[sweep, 0]),
            (lane_out.at[sweep, 1], lane_in.at[sweep, 1]),
        )
        return [
            pltpu.make_async_remote_copy(
                src, dst, halo_send.at[sweep, n], halo_recv.at[sweep, n],
                device_id=neighbours[n], device_id_type=MESH,
            )
            for n, (src, dst) in enumerate(pairs)
        ]

    def start_tangent_halo(sweep):
        copies = halo_copies(
            sweep, (fields[sweep].at[:, 16, pl.ds(8, 128), :], fields[sweep].at[:, 1, pl.ds(8, 128), :])
        )
        for f in range(2):
            lane_out[sweep, 0, 16 * f : 16 * f + 16, :] = flat_fields[sweep][edge_row(f, 127), :]
            lane_out[sweep, 1, 16 * f : 16 * f + 16, :] = flat_fields[sweep][edge_row(f, 0), :]
        for copy in copies[2:] + copies[:2]:
            copy.start()
        return copies

    def add_lanes(sweep, target, first, count):
        for f in range(2):
            for side, j, present in ((0, 0, has_left), (1, 127, has_right)):
                arrived = lane_in[sweep, side, 16 * f + first : 16 * f + first + count, :] * present
                if sweep < 2:
                    w = flat_wind_y[pl.ds(first * PAD + 8 + j, count, stride=PAD), :]
                    arrived = arrived * (0.1 + w if side == 0 else 0.1 - w)
                rows = edge_row(f, j, first, count)
                flat_fields[target][rows, :] = flat_fields[target][rows, :] + arrived

    def take_rows(sweep, copies):
        copies[0].wait_recv()
        copies[1].wait_recv()

        @pl.when(gx == 0)
        def _():
            fields[sweep][:, 0, 8:136, :] = jnp.zeros((2, 128, 128), F32)

        @pl.when(gx == 7)
        def _():
            fields[sweep][:, 17, 8:136, :] = jnp.zeros((2, 128, 128), F32)

    def pack_top(sweep, part, field, i, blocks=range(16)):
        for f in range(2):
            rows = pl.ds(f * 16 + (i >> 3) * 8, 8)
            packed = top_out[sweep, part, rows, :]
            base = (i & 7) * 16
            for n in blocks:
                level = fields[field][f, i + 1, 8 + 8 * n : 16 + 8 * n, 0:1]
                packed = jnp.where(lane_8 == base + n, jnp.broadcast_to(level, (8, 128)), packed)
            top_out[sweep, part, rows, :] = packed

    def top_copy(sweep, part):
        return pltpu.make_async_remote_copy(
            top_out.at[sweep, part], top_in.at[sweep, part], top_send.at[sweep, part], top_recv.at[sweep, part],
            device_id=partner, device_id_type=MESH,
        )

    def couple(sweep, part, field, i, transposed, runs=((0, 8), (8, 16))):
        for f in range(2):
            rows = pl.ds(f * 16 + (i >> 3) * 8, 8)
            packed = pltpu.roll(top_in[sweep, part, rows, :], (128 - (i & 7) * 16) & 127, 1)
            for first, last in runs:
                inner = slice(8 + 8 * first, 8 + 8 * last)
                own = fields[field][f, i + 1, inner, :]
                peer = jnp.concatenate(
                    [packed if n == 0 else pltpu.roll(packed, 128 - n, 1) for n in range(first, last)], axis=0
                )
                rate = exchange[i, 8 * first : 8 * last, :]
                if transposed:
                    value = own - rate * (own_share * own - peer_share * peer)
                else:
                    value = own - rate * (own_share * (own - peer))
                fields[field][f, i + 1, inner, :] = value

    def vertical(here):
        above = jnp.where(lane == 127, here, pltpu.roll(here, 127, 1))
        below = jnp.where(lane == 0, here, pltpu.roll(here, 1, 1))
        return 0.3 * here + 0.15 * (above + below)

    def neighbourhood(field, f, i, low):
        here = field[f, i + 1, low : low + BLOCK, :]
        up = field[f, i + 2, low : low + BLOCK, :]
        down = field[f, i, low : low + BLOCK, :]
        right = field[f, i + 1, low + 1 : low + 1 + BLOCK, :]
        left = field[f, i + 1, low - 1 : low - 1 + BLOCK, :]
        return here, up, down, right, left

    def tangent_row(sweep, target, i):
        for block in range(128 // BLOCK):
            low = 8 + block * BLOCK
            u = wind_x[i + 1, block * BLOCK : (block + 1) * BLOCK, :]
            w = wind_y[i, low : low + BLOCK, :]
            for f in range(2):
                here, up, down, right, left = neighbourhood(fields[sweep], f, i, low)
                fields[target][f, i + 1, low : low + BLOCK, :] = (
                    vertical(here) + 0.1 * ((up + down) + (right + left)) - (u * (up - down) + w * (right - left))
                )

    def adjoint_row(sweep, target, i):
        for block in range(128 // BLOCK):
            low = 8 + block * BLOCK
            inner = slice(block * BLOCK, (block + 1) * BLOCK)
            from_down = 0.1 - wind_x[i, inner, :]
            from_up = 0.1 + wind_x[i + 2, inner, :]
            from_left = 0.1 - wind_y[i, low - 1 : low - 1 + BLOCK, :]
            from_right = 0.1 + wind_y[i, low + 1 : low + 1 + BLOCK, :]
            for f in range(2):
                here, up, down, right, left = neighbourhood(fields[sweep], f, i, low)
                fields[target][f, i + 1, low : low + BLOCK, :] = (
                    vertical(here) + (from_down * down + from_up * up) + (from_left * left + from_right * right)
                )

    def each(body, low=0, high=16):
        def step(i, _):
            body(i)
            return 0

        lax.fori_loop(low, high, step, 0)

    for load in loads[:4]:
        load.wait()
    owner = owner_ref[...]
    owner_gx, owner_gy = owner >> 4, owner & 15
    owner_x, owner_y, owner_z = owner_gy >> 2, owner_gx >> 1, ((owner_gy & 3) << 1) | (owner_gx & 1)
    relative = ((owner_y - y + 4) & 3) * 32 + ((owner_x - x + 4) & 3) * 8 + ((owner_z - z + 8) & 7)
    tile_iota = lax.broadcasted_iota(jnp.int32, (128, 512), 0)
    hits = jnp.where(tile_iota == relative, 1.0, 0.0)
    hits_narrow = hits.astype(BF16)
    earlier = jnp.where(
        lax.broadcasted_iota(jnp.int32, (512, 512), 0) < lax.broadcasted_iota(jnp.int32, (512, 512), 1), 1.0, 0.0
    ).astype(BF16)
    slot = jnp.sum(matmul(hits_narrow, earlier) * hits, axis=0, keepdims=True).astype(jnp.int32)
    position = relative * 8 + slot
    column = column_ref[...]
    in_row = tile_iota == (relative & 15) * 8 + slot
    column_high = jnp.where(in_row, (column >> 7).astype(F32), 0.0).astype(BF16)
    column_low = jnp.where(in_row, (column & 127).astype(F32), 0.0).astype(BF16)
    send[:, 16, :] = 128.0 * matmul_nt(hits_narrow, column_high) + matmul_nt(hits_narrow, column_low)
    scale_high, scale_low = split(jnp.broadcast_to(jnp.sqrt(prec_ref[...]), (128, 512)))
    ops_high, ops_low = split(ops[...])

    def pack(chunk, _):
        slots = lax.broadcasted_iota(jnp.int32, (256, 512), 0) + chunk * 256
        pick = jnp.where(slots == position, 1.0, 0.0).astype(BF16)
        scale = matmul_nt(pick, scale_high) + matmul_nt(pick, scale_low)
        rows = matmul(pick, ops_high) + matmul(pick, ops_low)
        target = pl.ds(chunk * GROUP, GROUP)
        send[target, 0:8, :] = (rows[:, :128] * scale).reshape(GROUP, 8, 128)
        send[target, 8:16, :] = (rows[:, 128:] * scale).reshape(GROUP, 8, 128)
        return 0

    lax.fori_loop(0, CHUNKS, pack, 0)

    top_out[...] = jnp.zeros((4, 2, 32, 128), F32)
    for flat in flat_fields:
        for f in range(2):
            for j in (-1, 128):
                flat[edge_row(f, j), :] = jnp.zeros((16, 128), F32)

    loads[4].wait()

    def turn_state(i):
        for f in range(2):
            field_0[f, i + 1, 8:136, :] = flat_native[pl.ds(f * 2048 + i, 128, stride=16), :].T

    pl.semaphore_wait(barrier, 27)
    for step in range(1, 8):
        greet(line_sem, device(x, y, (z + step) & 7))
    each(turn_state)
    first_halo = start_tangent_halo(0)
    pl.semaphore_wait(line_sem, 7)

    pltpu.make_async_copy(send.at[0], recv.at[0], a2a_recv.at[0]).start()

    def dispatch(s, _):
        target = device((x + ((s >> 3) & 3)) & 3, (y + (s >> 5)) & 3, (z + (s & 7)) & 7)
        pltpu.make_async_remote_copy(
            send.at[s], recv.at[s], a2a_send, a2a_recv.at[s >> 5], device_id=target, device_id_type=MESH,
        ).start()
        return 0

    lax.fori_loop(1, 64, dispatch, 0)

    loads[5].wait()
    loads[6].wait()
    wind_x[0] = jnp.full((128, 128), -0.9, F32)
    wind_x[17] = jnp.full((128, 128), 0.9, F32)

    def turn_winds(i):
        wind_x[i + 1] = 0.5 * flat_winds[pl.ds(i, 128, stride=16), :].T
        wind_y[i, 8:136, :] = 0.5 * flat_winds[pl.ds(2048 + i, 128, stride=16), :].T
        wind_y[i, 0:8, :] = jnp.full((8, 128), -0.9, F32)
        wind_y[i, 136:144, :] = jnp.full((8, 128), 0.9, F32)
        rate = jnp.broadcast_to(gamma_ref[pl.ds(i, 1), :], (128, 128)).T
        exchange[i] = jnp.where(lax.broadcasted_iota(jnp.int32, (128, 128), 1) == 0, rate, 0.0)

    each(turn_winds)

    tops = []

    def sweep_rows(sweep, copies, compute, target, meet, after):
        each(compute, 1, 15)
        copies[2].wait_recv()
        copies[3].wait_recv()
        add_lanes(sweep, target, 0, 16)
        if meet is not None:
            each(lambda i: pack_top(meet, 0, target, i), 1, 15)
            inner = top_copy(meet, 0)
            inner.start()
            tops.append(inner)
            inner.wait_recv()
        each(lambda i: after(i, 0), 1, 15)
        take_rows(sweep, copies)
        for i in (0, 15):
            compute(i)
            add_lanes(sweep, target, i, 1)
            if meet is not None:
                pack_top(meet, 1, target, i)
        if meet is not None:
            outer = top_copy(meet, 1)
            outer.start()
            tops.append(outer)
            outer.wait_recv()
        for i in (0, 15):
            after(i, 1)

    sweep_rows(
        0, first_halo, lambda i: tangent_row(0, 1, i), 1, 0, lambda i, part: couple(0, part, 1, i, False)
    )
    second_halo = start_tangent_halo(1)
    lax.fori_loop(64, 128, dispatch, 0)

    def finish_second(i, part):
        couple(1, part, 2, i, False)
        for f in range(2):
            high, low = split(field_2[f, i + 1, 8:136, :])
            second[pl.ds(i * 128, 128), 128 * f : 128 * f + 128] = high
            second[pl.ds(i * 128, 128), 256 + 128 * f : 384 + 128 * f] = low
            field_2[f, i + 1, 8:136, :] = jnp.zeros((128, 128), F32)

    sweep_rows(1, second_halo, lambda i: tangent_row(1, 2, i), 2, 1, finish_second)
    for copy in second_halo:
        copy.wait_send()

    def observe(chunk, _):
        arrived = recv.at[pl.ds(chunk * GROUP, GROUP)]
        pltpu.make_async_copy(arrived, arrived, a2a_recv.at[chunk]).wait()
        group = pl.ds(chunk * GROUP, GROUP)
        where = jnp.concatenate(
            [
                jnp.sum(recv[pl.ds(chunk * GROUP, 16), 16, :], axis=0, keepdims=True),
                jnp.sum(recv[pl.ds(chunk * GROUP + 16, 16), 16, :], axis=0, keepdims=True),
            ],
            axis=1,
        ).astype(jnp.int32)
        down_rows = jnp.broadcast_to(where, (128, 256)).T
        within = lax.broadcasted_iota(jnp.int32, (256, 128), 1)
        for i in range(16):
            pick_cell[:, 128 * i : 128 * i + 128] = jnp.where(down_rows == within + 128 * i, 1.0, 0.0).astype(BF16)
        both = matmul(pick_cell[...], second[...])
        sampled = both[:, :256] + both[:, 256:]
        weights = jnp.concatenate(
            [recv[group, 0:8, :].reshape(256, 128), recv[group, 8:16, :].reshape(256, 128)], axis=1
        )
        spread = jnp.concatenate(split(weights * jnp.sum(sampled * weights, axis=1, keepdims=True)), axis=0)

        def scatter(quarter):
            cell = lax.broadcasted_iota(jnp.int32, (512, 256), 0) + quarter * 512
            pick = jnp.where(cell == where, 1.0, 0.0).astype(BF16)
            added = matmul(jnp.concatenate([pick, pick], axis=1), spread)
            for r in range(4):
                for f in range(2):
                    field_2[f, quarter * 4 + r + 1, 8:136, :] += added[
                        128 * r : 128 * r + 128, 128 * f : 128 * f + 128
                    ]

        each(scatter, 0, 4)
        return 0

    lax.fori_loop(0, CHUNKS, observe, 0)

    def start_adjoint_halo(sweep):
        copies = halo_copies(sweep, (row_out.at[sweep - 2, 0], row_out.at[sweep - 2, 1]))
        right = 0.1 - flat_wind_y[pl.ds(8 + 127, 16, stride=PAD), :]
        left = 0.1 + flat_wind_y[pl.ds(8, 16, stride=PAD), :]
        for f in range(2):
            lane_out[sweep, 0, 16 * f : 16 * f + 16, :] = right * flat_fields[sweep][edge_row(f, 127), :]
            lane_out[sweep, 1, 16 * f : 16 * f + 16, :] = left * flat_fields[sweep][edge_row(f, 0), :]
        copies[2].start()
        copies[3].start()
        for f in range(2):
            row_out[sweep - 2, 0, f] = (0.1 - wind_x[16]) * fields[sweep][f, 16, 8:136, :]
        copies[0].start()
        for f in range(2):
            row_out[sweep - 2, 1, f] = (0.1 + wind_x[1]) * fields[sweep][f, 1, 8:136, :]
        copies[1].start()
        return copies

    for i in (0, 15):
        pack_top(2, 1, 2, i)
    each(lambda i: pack_top(2, 1, 2, i, (0, 15)), 1, 15)
    outer_top = top_copy(2, 1)
    outer_top.start()
    each(lambda i: pack_top(2, 0, 2, i, range(1, 15)), 1, 15)
    inner_top = top_copy(2, 0)
    inner_top.start()
    outer_top.wait_recv()
    for i in (0, 15):
        couple(2, 1, 2, i, True)
    each(lambda i: couple(2, 1, 2, i, True, ((0, 1), (15, 16))), 1, 15)
    third_halo = start_adjoint_halo(2)
    inner_top.wait_recv()
    each(lambda i: couple(2, 0, 2, i, True, ((1, 8), (8, 15))), 1, 15)
    sweep_rows(2, third_halo, lambda i: adjoint_row(2, 3, i), 3, 3, lambda i, part: couple(3, part, 3, i, True))
    fourth_halo = start_adjoint_halo(3)

    def turn_back(i, part):
        for f in range(2):
            flat_native[pl.ds(f * 2048 + i, 128, stride=16), :] = field_1[f, i + 1, 8:136, :].T

    sweep_rows(3, fourth_halo, lambda i: adjoint_row(3, 1, i), 1, None, turn_back)
    started = tops + [outer_top, inner_top] + first_halo + third_halo + fourth_halo
    store = pltpu.make_async_copy(native, out_hbm, store_sem)
    store.start()
    for copy in started:
        copy.wait_send()
    sent = recv.at[pl.ds(1, 127)]
    pltpu.make_async_copy(sent, sent, a2a_send).wait()
    store.wait()


def local(state_incr, winds, coupling, background, obs_dest, obs_col, obs_op, obs_prec):
    shape = state_incr.shape[1:]
    tile = (shape[0] * shape[1],) + shape[2:]
    hbm = pl.BlockSpec(memory_space=pltpu.HBM)
    adjoint = pl.pallas_call(
        kernel,
        out_shape=jax.ShapeDtypeStruct(tile, F32),
        in_specs=[hbm] * 7,
        out_specs=pl.BlockSpec(memory_space=pl.ANY),
        scratch_shapes=[
            pltpu.VMEM((1, 512), jnp.int32),
            pltpu.VMEM((1, 512), jnp.int32),
            pltpu.VMEM((1, 512), F32),
            pltpu.VMEM((16, 128), F32),
            pltpu.VMEM(tile, F32),
            pltpu.VMEM(tile, F32),
            pltpu.VMEM((2, 18, PAD, 128), F32),
            pltpu.VMEM((2, 18, PAD, 128), F32),
            pltpu.VMEM((2, 18, PAD, 128), F32),
            pltpu.VMEM((2, 18, PAD, 128), F32),
            pltpu.VMEM((18, 128, 128), F32),
            pltpu.VMEM((16, PAD, 128), F32),
            pltpu.VMEM((16, 128, 128), F32),
            pltpu.VMEM((512, 256), F32),
            pltpu.VMEM((128, 17, 128), F32),
            pltpu.VMEM((128, 17, 128), F32),
            pltpu.VMEM((2, 2, 2, 128, 128), F32),
            pltpu.VMEM((4, 2, 32, 128), F32),
            pltpu.VMEM((4, 2, 32, 128), F32),
            pltpu.VMEM((4, 2, 32, 128), F32),
            pltpu.VMEM((4, 2, 32, 128), F32),
            pltpu.VMEM((2048, 512), BF16),
            pltpu.VMEM((256, 2048), BF16),
            pltpu.SemaphoreType.DMA((7,)),
            pltpu.SemaphoreType.DMA,
            pltpu.SemaphoreType.DMA,
            pltpu.SemaphoreType.DMA((CHUNKS,)),
            pltpu.SemaphoreType.DMA((4, 4)),
            pltpu.SemaphoreType.DMA((4, 4)),
            pltpu.SemaphoreType.DMA((4, 2)),
            pltpu.SemaphoreType.DMA((4, 2)),
            pltpu.SemaphoreType.REGULAR,
        ],
        compiler_params=pltpu.CompilerParams(
            collective_id=0, has_side_effects=True, vmem_limit_bytes=60 * 1024 * 1024
        ),
    )(
        state_incr.reshape(tile), winds.reshape(tile), obs_op,
        obs_dest.reshape(1, -1), obs_col.reshape(1, -1), obs_prec.reshape(1, -1), coupling,
    )
    result = background[0][:, :, None, None] * state_incr[0] + adjoint.reshape(shape)
    return result[None]


def solution(mesh):
    placed = (
        P("comp", None, None, "gx", "gy"),
        P("comp", None, None, "gx", "gy"),
        P("gx", "gy"),
        P("comp", None, None),
        P(("comp", "gx", "gy"), None),
        P(("comp", "gx", "gy")),
        P(("comp", "gx", "gy"), None),
        P(("comp", "gx", "gy")),
    )
    return jax.shard_map(
        local,
        mesh=mesh,
        in_specs=placed,
        out_specs=P("comp", None, None, "gx", "gy"),
        check_vma=False,
    )
```

```python
import jax
import jax.numpy as jnp
from jax import lax
from jax.experimental import pallas as pl
from jax.experimental.pallas import tpu as pltpu
from jax.sharding import PartitionSpec as P

MESH = pl.DeviceIdType.MESH
F32 = jnp.float32
BF16 = jnp.bfloat16
CHUNKS = 4
GROUP = 32
PAD = 144
BLOCK = 32


def device(x, y, z):
    return {"gx": y * 2 + (z & 1), "gy": x * 4 + (z >> 1)}


def split(value):
    high = value.astype(BF16)
    return high, (value - high.astype(F32)).astype(BF16)


def matmul(a, b):
    return lax.dot_general(a, b, (((1,), (0,)), ((), ())), preferred_element_type=F32)


def matmul_nt(a, b):
    return lax.dot_general(a, b, (((1,), (1,)), ((), ())), preferred_element_type=F32)


def kernel(
    state_hbm, winds_hbm, op_hbm, owner_hbm, column_hbm, prec_hbm, gamma_hbm, precision_hbm, out_ref,
    owner_ref, column_ref, prec_ref, gamma_ref, precision_ref, native, native_winds, field_0, field_1, field_2, field_3, wind_x, wind_y, exchange, ops, send, recv,
    row_out, lane_out, lane_in, top_out, top_in,
    second, pick_cell,
    load_sem, a2a_send, a2a_recv, halo_send, halo_recv, top_send, top_recv, line_sem,
):
    comp = lax.axis_index("comp")
    gx = lax.axis_index("gx")
    gy = lax.axis_index("gy")
    x, y, z = gy >> 2, gx >> 1, ((gy & 3) << 1) | (gx & 1)

    loads = [
        pltpu.make_async_copy(src, dst, load_sem.at[n])
        for n, (src, dst) in enumerate(
            (
                (owner_hbm, owner_ref), (column_hbm, column_ref), (prec_hbm, prec_ref), (op_hbm, ops),
                (state_hbm, native), (winds_hbm, native_winds), (gamma_hbm, gamma_ref), (precision_hbm, precision_ref),
            )
        )
    ]
    for load in loads:
        load.start()

    neighbours = (
        {"gx": (gx + 1) & 7},
        {"gx": (gx + 7) & 7},
        {"gy": (gy + 1) & 15},
        {"gy": (gy + 15) & 15},
    )
    partner = {"comp": 1 - comp}
    barrier = pltpu.get_barrier_semaphore()

    def greet(semaphore, target):
        pl.semaphore_signal(semaphore, inc=1, device_id=target, device_id_type=MESH)

    for target in neighbours:
        greet(barrier, target)
    greet(barrier, partner)
    for step in range(1, 8):
        greet(barrier, device(x, y, (z + step) & 7))
    for step in range(1, 16):
        greet(barrier, device((x + step) & 3, (y + step // 4) & 3, z))

    lane = lax.broadcasted_iota(jnp.int32, (BLOCK, 128), 1)
    lane_8 = lax.broadcasted_iota(jnp.int32, (8, 128), 1)
    has_left = jnp.where(gy > 0, 1.0, 0.0)
    has_right = jnp.where(gy < 15, 1.0, 0.0)
    own_share = jnp.where(comp == 0, 1.0, 0.5)
    peer_share = 1.5 - own_share
    fields = (field_0, field_1, field_2, field_3)
    flat_fields = [field.reshape(2 * 18 * PAD, 128) for field in fields]
    flat_native = native.reshape(4096, 128)
    flat_out = out_ref.reshape(4096, 128)
    flat_winds = native_winds.reshape(4096, 128)
    flat_wind_y = wind_y.reshape(16 * PAD, 128)

    def edge_row(f, j, first=0, count=16):
        return pl.ds((f * 18 + 1 + first) * PAD + 8 + j, count, stride=PAD)

    def halo_copies(sweep, sources):
        pairs = (
            (sources[0], fields[sweep].at[:, 0, pl.ds(8, 128), :]),
            (sources[1], fields[sweep].at[:, 17, pl.ds(8, 128), :]),
            (lane_out.at[sweep, 0], lane_in.at[sweep, 0]),
            (lane_out.at[sweep, 1], lane_in.at[sweep, 1]),
        )
        return [
            pltpu.make_async_remote_copy(
                src, dst, halo_send.at[sweep, n], halo_recv.at[sweep, n],
                device_id=neighbours[n], device_id_type=MESH,
            )
            for n, (src, dst) in enumerate(pairs)
        ]

    def start_tangent_halo(sweep):
        copies = halo_copies(
            sweep, (fields[sweep].at[:, 16, pl.ds(8, 128), :], fields[sweep].at[:, 1, pl.ds(8, 128), :])
        )
        for f in range(2):
            lane_out[sweep, 0, 16 * f : 16 * f + 16, :] = flat_fields[sweep][edge_row(f, 127), :]
            lane_out[sweep, 1, 16 * f : 16 * f + 16, :] = flat_fields[sweep][edge_row(f, 0), :]
        for copy in copies[2:] + copies[:2]:
            copy.start()
        return copies

    def add_lanes(sweep, target, first, count):
        for f in range(2):
            for side, j, present in ((0, 0, has_left), (1, 127, has_right)):
                arrived = lane_in[sweep, side, 16 * f + first : 16 * f + first + count, :] * present
                if sweep < 2:
                    w = flat_wind_y[pl.ds(first * PAD + 8 + j, count, stride=PAD), :]
                    arrived = arrived * (0.1 + w if side == 0 else 0.1 - w)
                rows = edge_row(f, j, first, count)
                flat_fields[target][rows, :] = flat_fields[target][rows, :] + arrived

    def take_rows(sweep, copies):
        copies[0].wait_recv()
        copies[1].wait_recv()

        @pl.when(gx == 0)
        def _():
            fields[sweep][:, 0, 8:136, :] = jnp.zeros((2, 128, 128), F32)

        @pl.when(gx == 7)
        def _():
            fields[sweep][:, 17, 8:136, :] = jnp.zeros((2, 128, 128), F32)

    def pack_top(sweep, part, field, i, blocks=range(16)):
        for f in range(2):
            rows = pl.ds(f * 16 + (i >> 3) * 8, 8)
            packed = top_out[sweep, part, rows, :]
            base = (i & 7) * 16
            for n in blocks:
                level = fields[field][f, i + 1, 8 + 8 * n : 16 + 8 * n, 0:1]
                packed = jnp.where(lane_8 == base + n, jnp.broadcast_to(level, (8, 128)), packed)
            top_out[sweep, part, rows, :] = packed

    def top_copy(sweep, part):
        return pltpu.make_async_remote_copy(
            top_out.at[sweep, part], top_in.at[sweep, part], top_send.at[sweep, part], top_recv.at[sweep, part],
            device_id=partner, device_id_type=MESH,
        )

    def couple(sweep, part, field, i, transposed, runs=((0, 8), (8, 16))):
        for f in range(2):
            rows = pl.ds(f * 16 + (i >> 3) * 8, 8)
            packed = pltpu.roll(top_in[sweep, part, rows, :], (128 - (i & 7) * 16) & 127, 1)
            for first, last in runs:
                inner = slice(8 + 8 * first, 8 + 8 * last)
                own = fields[field][f, i + 1, inner, :]
                peer = jnp.concatenate(
                    [packed if n == 0 else pltpu.roll(packed, 128 - n, 1) for n in range(first, last)], axis=0
                )
                rate = exchange[i, 8 * first : 8 * last, :]
                if transposed:
                    value = own - rate * (own_share * own - peer_share * peer)
                else:
                    value = own - rate * (own_share * (own - peer))
                fields[field][f, i + 1, inner, :] = value

    def vertical(here):
        above = jnp.where(lane == 127, here, pltpu.roll(here, 127, 1))
        below = jnp.where(lane == 0, here, pltpu.roll(here, 1, 1))
        return 0.3 * here + 0.15 * (above + below)

    def neighbourhood(field, f, i, low):
        here = field[f, i + 1, low : low + BLOCK, :]
        up = field[f, i + 2, low : low + BLOCK, :]
        down = field[f, i, low : low + BLOCK, :]
        right = field[f, i + 1, low + 1 : low + 1 + BLOCK, :]
        left = field[f, i + 1, low - 1 : low - 1 + BLOCK, :]
        return here, up, down, right, left

    def tangent_row(sweep, target, i):
        for block in range(128 // BLOCK):
            low = 8 + block * BLOCK
            u = wind_x[i + 1, block * BLOCK : (block + 1) * BLOCK, :]
            w = wind_y[i, low : low + BLOCK, :]
            for f in range(2):
                here, up, down, right, left = neighbourhood(fields[sweep], f, i, low)
                fields[target][f, i + 1, low : low + BLOCK, :] = (
                    vertical(here) + 0.1 * ((up + down) + (right + left)) - (u * (up - down) + w * (right - left))
                )

    def adjoint_row(sweep, target, i):
        for block in range(128 // BLOCK):
            low = 8 + block * BLOCK
            inner = slice(block * BLOCK, (block + 1) * BLOCK)
            from_down = 0.1 - wind_x[i, inner, :]
            from_up = 0.1 + wind_x[i + 2, inner, :]
            from_left = 0.1 - wind_y[i, low - 1 : low - 1 + BLOCK, :]
            from_right = 0.1 + wind_y[i, low + 1 : low + 1 + BLOCK, :]
            for f in range(2):
                here, up, down, right, left = neighbourhood(fields[sweep], f, i, low)
                fields[target][f, i + 1, low : low + BLOCK, :] = (
                    vertical(here) + (from_down * down + from_up * up) + (from_left * left + from_right * right)
                )

    def each(body, low=0, high=16):
        def step(i, _):
            body(i)
            return 0

        lax.fori_loop(low, high, step, 0, unroll=2)

    for load in loads[:4]:
        load.wait()
    owner = owner_ref[...]
    owner_gx, owner_gy = owner >> 4, owner & 15
    owner_x, owner_y, owner_z = owner_gy >> 2, owner_gx >> 1, ((owner_gy & 3) << 1) | (owner_gx & 1)
    relative = ((owner_y - y + 4) & 3) * 32 + ((owner_x - x + 4) & 3) * 8 + ((owner_z - z + 8) & 7)
    tile_iota = lax.broadcasted_iota(jnp.int32, (128, 512), 0)
    hits = jnp.where(tile_iota == relative, 1.0, 0.0)
    hits_narrow = hits.astype(BF16)
    earlier = jnp.where(
        lax.broadcasted_iota(jnp.int32, (512, 512), 0) < lax.broadcasted_iota(jnp.int32, (512, 512), 1), 1.0, 0.0
    ).astype(BF16)
    slot = jnp.sum(matmul(hits_narrow, earlier) * hits, axis=0, keepdims=True).astype(jnp.int32)
    position = relative * 8 + slot
    column = column_ref[...]
    in_row = tile_iota == (relative & 15) * 8 + slot
    column_high = jnp.where(in_row, (column >> 7).astype(F32), 0.0).astype(BF16)
    column_low = jnp.where(in_row, (column & 127).astype(F32), 0.0).astype(BF16)
    send[:, 16, :] = 128.0 * matmul_nt(hits_narrow, column_high) + matmul_nt(hits_narrow, column_low)
    scale_high, scale_low = split(jnp.broadcast_to(jnp.sqrt(prec_ref[...]), (128, 512)))
    ops_high, ops_low = split(ops[...])

    def pack(chunk, _):
        slots = lax.broadcasted_iota(jnp.int32, (256, 512), 0) + chunk * 256
        pick = jnp.where(slots == position, 1.0, 0.0).astype(BF16)
        scale = matmul_nt(pick, scale_high) + matmul_nt(pick, scale_low)
        rows = matmul(pick, ops_high) + matmul(pick, ops_low)
        target = pl.ds(chunk * GROUP, GROUP)
        send[target, 0:8, :] = (rows[:, :128] * scale).reshape(GROUP, 8, 128)
        send[target, 8:16, :] = (rows[:, 128:] * scale).reshape(GROUP, 8, 128)
        return 0

    lax.fori_loop(0, CHUNKS, pack, 0)

    top_out[...] = jnp.zeros((4, 2, 32, 128), F32)
    for flat in flat_fields:
        for f in range(2):
            for j in (-1, 128):
                flat[edge_row(f, j), :] = jnp.zeros((16, 128), F32)

    loads[4].wait()

    def turn_state(i):
        for f in range(2):
            field_0[f, i + 1, 8:136, :] = flat_native[pl.ds(f * 2048 + i, 128, stride=16), :].T

    pl.semaphore_wait(barrier, 27)
    for step in range(1, 8):
        greet(line_sem, device(x, y, (z + step) & 7))
    each(turn_state)
    first_halo = start_tangent_halo(0)
    pl.semaphore_wait(line_sem, 7)

    pltpu.make_async_copy(send.at[0], recv.at[0], a2a_recv.at[0]).start()

    def dispatch(s, _):
        target = device((x + ((s >> 3) & 3)) & 3, (y + (s >> 5)) & 3, (z + (s & 7)) & 7)
        pltpu.make_async_remote_copy(
            send.at[s], recv.at[s], a2a_send, a2a_recv.at[s >> 5], device_id=target, device_id_type=MESH,
        ).start()
        return 0

    lax.fori_loop(1, 32, dispatch, 0)

    loads[5].wait()
    loads[6].wait()
    loads[7].wait()
    wind_x[0] = jnp.full((128, 128), -0.9, F32)
    wind_x[17] = jnp.full((128, 128), 0.9, F32)

    def turn_winds(i):
        wind_x[i + 1] = 0.5 * flat_winds[pl.ds(i, 128, stride=16), :].T
        wind_y[i, 8:136, :] = 0.5 * flat_winds[pl.ds(2048 + i, 128, stride=16), :].T
        wind_y[i, 0:8, :] = jnp.full((8, 128), -0.9, F32)
        wind_y[i, 136:144, :] = jnp.full((8, 128), 0.9, F32)
        rate = jnp.broadcast_to(gamma_ref[pl.ds(i, 1), :], (128, 128)).T
        exchange[i] = jnp.where(lax.broadcasted_iota(jnp.int32, (128, 128), 1) == 0, rate, 0.0)

    each(turn_winds)

    tops = []

    def sweep_rows(sweep, copies, compute, target, meet, after):
        each(compute, 1, 15)
        copies[2].wait_recv()
        copies[3].wait_recv()
        add_lanes(sweep, target, 0, 16)
        if meet is not None:
            each(lambda i: pack_top(meet, 0, target, i), 1, 15)
            inner = top_copy(meet, 0)
            inner.start()
            tops.append(inner)
            inner.wait_recv()
        each(lambda i: after(i, 0), 1, 15)
        take_rows(sweep, copies)
        for i in (0, 15):
            compute(i)
            add_lanes(sweep, target, i, 1)
            if meet is not None:
                pack_top(meet, 1, target, i)
        if meet is not None:
            outer = top_copy(meet, 1)
            outer.start()
            tops.append(outer)
            outer.wait_recv()
        for i in (0, 15):
            after(i, 1)

    precision = [jnp.broadcast_to(precision_ref[f : f + 1, :], (128, 128)).T for f in range(2)]

    def scale_state(i):
        for f in range(2):
            rows = pl.ds(f * 2048 + i, 128, stride=16)
            flat_out[rows, :] = precision[f] * flat_native[rows, :]

    each(scale_state)
    sweep_rows(
        0, first_halo, lambda i: tangent_row(0, 1, i), 1, 0, lambda i, part: couple(0, part, 1, i, False)
    )
    second_halo = start_tangent_halo(1)
    lax.fori_loop(32, 128, dispatch, 0)

    def finish_second(i, part):
        couple(1, part, 2, i, False)
        for f in range(2):
            high, low = split(field_2[f, i + 1, 8:136, :])
            second[pl.ds(i * 128, 128), 128 * f : 128 * f + 128] = high
            second[pl.ds(i * 128, 128), 256 + 128 * f : 384 + 128 * f] = low
            field_2[f, i + 1, 8:136, :] = jnp.zeros((128, 128), F32)

    sweep_rows(1, second_halo, lambda i: tangent_row(1, 2, i), 2, 1, finish_second)
    for copy in second_halo:
        copy.wait_send()

    def observe(chunk, _):
        arrived = recv.at[pl.ds(chunk * GROUP, GROUP)]
        pltpu.make_async_copy(arrived, arrived, a2a_recv.at[chunk]).wait()
        group = pl.ds(chunk * GROUP, GROUP)
        where = jnp.concatenate(
            [
                jnp.sum(recv[pl.ds(chunk * GROUP, 16), 16, :], axis=0, keepdims=True),
                jnp.sum(recv[pl.ds(chunk * GROUP + 16, 16), 16, :], axis=0, keepdims=True),
            ],
            axis=1,
        ).astype(jnp.int32)
        down_rows = jnp.broadcast_to(where, (128, 256)).T
        within = lax.broadcasted_iota(jnp.int32, (256, 128), 1)
        for i in range(16):
            pick_cell[:, 128 * i : 128 * i + 128] = jnp.where(down_rows == within + 128 * i, 1.0, 0.0).astype(BF16)
        both = matmul(pick_cell[...], second[...])
        sampled = both[:, :256] + both[:, 256:]
        weights = jnp.concatenate(
            [recv[group, 0:8, :].reshape(256, 128), recv[group, 8:16, :].reshape(256, 128)], axis=1
        )
        spread = jnp.concatenate(split(weights * jnp.sum(sampled * weights, axis=1, keepdims=True)), axis=0)

        def scatter(quarter):
            cell = lax.broadcasted_iota(jnp.int32, (512, 256), 0) + quarter * 512
            pick = jnp.where(cell == where, 1.0, 0.0).astype(BF16)
            added = matmul(jnp.concatenate([pick, pick], axis=1), spread)
            for r in range(4):
                for f in range(2):
                    field_2[f, quarter * 4 + r + 1, 8:136, :] += added[
                        128 * r : 128 * r + 128, 128 * f : 128 * f + 128
                    ]

        each(scatter, 0, 4)
        return 0

    lax.fori_loop(0, CHUNKS, observe, 0)

    def start_adjoint_halo(sweep):
        copies = halo_copies(sweep, (row_out.at[sweep - 2, 0], row_out.at[sweep - 2, 1]))
        right = 0.1 - flat_wind_y[pl.ds(8 + 127, 16, stride=PAD), :]
        left = 0.1 + flat_wind_y[pl.ds(8, 16, stride=PAD), :]
        for f in range(2):
            lane_out[sweep, 0, 16 * f : 16 * f + 16, :] = right * flat_fields[sweep][edge_row(f, 127), :]
            lane_out[sweep, 1, 16 * f : 16 * f + 16, :] = left * flat_fields[sweep][edge_row(f, 0), :]
        copies[2].start()
        copies[3].start()
        for f in range(2):
            row_out[sweep - 2, 0, f] = (0.1 - wind_x[16]) * fields[sweep][f, 16, 8:136, :]
        copies[0].start()
        for f in range(2):
            row_out[sweep - 2, 1, f] = (0.1 + wind_x[1]) * fields[sweep][f, 1, 8:136, :]
        copies[1].start()
        return copies

    for i in (0, 15):
        pack_top(2, 1, 2, i)
    each(lambda i: pack_top(2, 1, 2, i, (0, 15)), 1, 15)
    outer_top = top_copy(2, 1)
    outer_top.start()
    each(lambda i: pack_top(2, 0, 2, i, range(1, 15)), 1, 15)
    inner_top = top_copy(2, 0)
    inner_top.start()
    outer_top.wait_recv()
    for i in (0, 15):
        couple(2, 1, 2, i, True)
    each(lambda i: couple(2, 1, 2, i, True, ((0, 1), (15, 16))), 1, 15)
    third_halo = start_adjoint_halo(2)
    inner_top.wait_recv()
    each(lambda i: couple(2, 0, 2, i, True, ((1, 8), (8, 15))), 1, 15)
    sweep_rows(2, third_halo, lambda i: adjoint_row(2, 3, i), 3, 3, lambda i, part: couple(3, part, 3, i, True))
    fourth_halo = start_adjoint_halo(3)

    def turn_back(i, part):
        for f in range(2):
            rows = pl.ds(f * 2048 + i, 128, stride=16)
            flat_out[rows, :] = flat_out[rows, :] + field_1[f, i + 1, 8:136, :].T

    sweep_rows(3, fourth_halo, lambda i: adjoint_row(3, 1, i), 1, None, turn_back)
    started = tops + [outer_top, inner_top] + first_halo + third_halo + fourth_halo
    for copy in started:
        copy.wait_send()
    sent = recv.at[pl.ds(1, 127)]
    pltpu.make_async_copy(sent, sent, a2a_send).wait()


def local(state_incr, winds, coupling, background, obs_dest, obs_col, obs_op, obs_prec):
    shape = state_incr.shape[1:]
    tile = (shape[0] * shape[1],) + shape[2:]
    hbm = pl.BlockSpec(memory_space=pltpu.HBM)
    result = pl.pallas_call(
        kernel,
        out_shape=pltpu.VMEM(tile, F32),
        in_specs=[hbm] * 8,
        out_specs=pl.BlockSpec(memory_space=pltpu.VMEM),
        scratch_shapes=[
            pltpu.VMEM((1, 512), jnp.int32),
            pltpu.VMEM((1, 512), jnp.int32),
            pltpu.VMEM((1, 512), F32),
            pltpu.VMEM((16, 128), F32),
            pltpu.VMEM((2, 128), F32),
            pltpu.VMEM(tile, F32),
            pltpu.VMEM(tile, F32),
            pltpu.VMEM((2, 18, PAD, 128), F32),
            pltpu.VMEM((2, 18, PAD, 128), F32),
            pltpu.VMEM((2, 18, PAD, 128), F32),
            pltpu.VMEM((2, 18, PAD, 128), F32),
            pltpu.VMEM((18, 128, 128), F32),
            pltpu.VMEM((16, PAD, 128), F32),
            pltpu.VMEM((16, 128, 128), F32),
            pltpu.VMEM((512, 256), F32),
            pltpu.VMEM((128, 17, 128), F32),
            pltpu.VMEM((128, 17, 128), F32),
            pltpu.VMEM((2, 2, 2, 128, 128), F32),
            pltpu.VMEM((4, 2, 32, 128), F32),
            pltpu.VMEM((4, 2, 32, 128), F32),
            pltpu.VMEM((4, 2, 32, 128), F32),
            pltpu.VMEM((4, 2, 32, 128), F32),
            pltpu.VMEM((2048, 512), BF16),
            pltpu.VMEM((256, 2048), BF16),
            pltpu.SemaphoreType.DMA((8,)),
            pltpu.SemaphoreType.DMA,
            pltpu.SemaphoreType.DMA((CHUNKS,)),
            pltpu.SemaphoreType.DMA((4, 4)),
            pltpu.SemaphoreType.DMA((4, 4)),
            pltpu.SemaphoreType.DMA((4, 2)),
            pltpu.SemaphoreType.DMA((4, 2)),
            pltpu.SemaphoreType.REGULAR,
        ],
        compiler_params=pltpu.CompilerParams(
            collective_id=0, has_side_effects=True, vmem_limit_bytes=60 * 1024 * 1024
        ),
    )(
        state_incr.reshape(tile), winds.reshape(tile), obs_op,
        obs_dest.reshape(1, -1), obs_col.reshape(1, -1), obs_prec.reshape(1, -1), coupling, background[0],
    )
    return result.reshape((1,) + shape)


def solution(mesh):
    placed = (
        P("comp", None, None, "gx", "gy"),
        P("comp", None, None, "gx", "gy"),
        P("gx", "gy"),
        P("comp", None, None),
        P(("comp", "gx", "gy"), None),
        P(("comp", "gx", "gy")),
        P(("comp", "gx", "gy"), None),
        P(("comp", "gx", "gy")),
    )
    return jax.shard_map(
        local,
        mesh=mesh,
        in_specs=placed,
        out_specs=P("comp", None, None, "gx", "gy"),
        check_vma=False,
    )
```

```python
import jax
import jax.numpy as jnp
from jax import lax
from jax.experimental import pallas as pl
from jax.experimental.pallas import tpu as pltpu
from jax.sharding import PartitionSpec as P

MESH = pl.DeviceIdType.MESH
F32 = jnp.float32
BF16 = jnp.bfloat16
CHUNKS = 4
GROUP = 32
PAD = 144
BLOCK = 32


def device(x, y, z):
    return {"gx": y * 2 + (z & 1), "gy": x * 4 + (z >> 1)}


def split(value):
    high = value.astype(BF16)
    return high, (value - high.astype(F32)).astype(BF16)


def matmul(a, b):
    return lax.dot_general(a, b, (((1,), (0,)), ((), ())), preferred_element_type=F32)


def matmul_nt(a, b):
    return lax.dot_general(a, b, (((1,), (1,)), ((), ())), preferred_element_type=F32)


def kernel(
    state_hbm, winds_hbm, op_hbm, owner_hbm, column_hbm, prec_hbm, gamma_hbm, precision_hbm, out_ref,
    owner_ref, column_ref, prec_ref, gamma_ref, precision_ref, native, native_winds, field_0, field_1, field_2, field_3, wind_x, wind_y, exchange, ops, send, recv,
    row_out, lane_out, lane_in, top_out, top_in,
    second, pick_cell,
    load_sem, a2a_send, a2a_recv, halo_send, halo_recv, top_send, top_recv, line_sem,
):
    comp = lax.axis_index("comp")
    gx = lax.axis_index("gx")
    gy = lax.axis_index("gy")
    x, y, z = gy >> 2, gx >> 1, ((gy & 3) << 1) | (gx & 1)

    loads = [
        pltpu.make_async_copy(src, dst, load_sem.at[n])
        for n, (src, dst) in enumerate(
            (
                (owner_hbm, owner_ref), (column_hbm, column_ref), (prec_hbm, prec_ref), (op_hbm, ops),
                (state_hbm, native), (winds_hbm, native_winds), (gamma_hbm, gamma_ref), (precision_hbm, precision_ref),
            )
        )
    ]
    for load in loads:
        load.start()

    neighbours = (
        {"gx": (gx + 1) & 7},
        {"gx": (gx + 7) & 7},
        {"gy": (gy + 1) & 15},
        {"gy": (gy + 15) & 15},
    )
    partner = {"comp": 1 - comp}
    barrier = pltpu.get_barrier_semaphore()

    def greet(semaphore, target):
        pl.semaphore_signal(semaphore, inc=1, device_id=target, device_id_type=MESH)

    for step in range(1, 8):
        greet(barrier, device(x, y, (z + step) & 7))
    for step in range(1, 16):
        greet(barrier, device((x + step) & 3, (y + step // 4) & 3, z))
    for target in neighbours:
        greet(barrier, target)
    greet(barrier, partner)

    lane = lax.broadcasted_iota(jnp.int32, (BLOCK, 128), 1)
    lane_8 = lax.broadcasted_iota(jnp.int32, (8, 128), 1)
    has_left = jnp.where(gy > 0, 1.0, 0.0)
    has_right = jnp.where(gy < 15, 1.0, 0.0)
    own_share = jnp.where(comp == 0, 1.0, 0.5)
    peer_share = 1.5 - own_share
    fields = (field_0, field_1, field_2, field_3)
    flat_fields = [field.reshape(2 * 18 * PAD, 128) for field in fields]
    flat_native = native.reshape(4096, 128)
    flat_out = out_ref.reshape(4096, 128)
    flat_winds = native_winds.reshape(4096, 128)
    flat_wind_y = wind_y.reshape(16 * PAD, 128)

    def edge_row(f, j, first=0, count=16):
        return pl.ds((f * 18 + 1 + first) * PAD + 8 + j, count, stride=PAD)

    def halo_copies(sweep, sources):
        pairs = (
            (sources[0], fields[sweep].at[:, 0, pl.ds(8, 128), :]),
            (sources[1], fields[sweep].at[:, 17, pl.ds(8, 128), :]),
            (lane_out.at[sweep, 0], lane_in.at[sweep, 0]),
            (lane_out.at[sweep, 1], lane_in.at[sweep, 1]),
        )
        return [
            pltpu.make_async_remote_copy(
                src, dst, halo_send.at[sweep, n], halo_recv.at[sweep, n],
                device_id=neighbours[n], device_id_type=MESH,
            )
            for n, (src, dst) in enumerate(pairs)
        ]

    def start_tangent_halo(sweep):
        copies = halo_copies(
            sweep, (fields[sweep].at[:, 16, pl.ds(8, 128), :], fields[sweep].at[:, 1, pl.ds(8, 128), :])
        )
        for f in range(2):
            lane_out[sweep, 0, 16 * f : 16 * f + 16, :] = flat_fields[sweep][edge_row(f, 127), :]
            lane_out[sweep, 1, 16 * f : 16 * f + 16, :] = flat_fields[sweep][edge_row(f, 0), :]
        for copy in copies[2:] + copies[:2]:
            copy.start()
        return copies

    def add_lanes(sweep, target, first, count):
        for f in range(2):
            for side, j, present in ((0, 0, has_left), (1, 127, has_right)):
                arrived = lane_in[sweep, side, 16 * f + first : 16 * f + first + count, :] * present
                if sweep < 2:
                    w = flat_wind_y[pl.ds(first * PAD + 8 + j, count, stride=PAD), :]
                    arrived = arrived * (0.1 + w if side == 0 else 0.1 - w)
                rows = edge_row(f, j, first, count)
                flat_fields[target][rows, :] = flat_fields[target][rows, :] + arrived

    def take_rows(sweep, copies):
        copies[0].wait_recv()
        copies[1].wait_recv()

        @pl.when(gx == 0)
        def _():
            fields[sweep][:, 0, 8:136, :] = jnp.zeros((2, 128, 128), F32)

        @pl.when(gx == 7)
        def _():
            fields[sweep][:, 17, 8:136, :] = jnp.zeros((2, 128, 128), F32)

    def pack_top(sweep, part, field, i, blocks=range(16)):
        for f in range(2):
            rows = pl.ds(f * 16 + (i >> 3) * 8, 8)
            packed = top_out[sweep, part, rows, :]
            base = (i & 7) * 16
            for n in blocks:
                level = fields[field][f, i + 1, 8 + 8 * n : 16 + 8 * n, 0:1]
                packed = jnp.where(lane_8 == base + n, jnp.broadcast_to(level, (8, 128)), packed)
            top_out[sweep, part, rows, :] = packed

    def top_copy(sweep, part):
        return pltpu.make_async_remote_copy(
            top_out.at[sweep, part], top_in.at[sweep, part], top_send.at[sweep, part], top_recv.at[sweep, part],
            device_id=partner, device_id_type=MESH,
        )

    def couple(sweep, part, field, i, transposed, runs=((0, 8), (8, 16))):
        for f in range(2):
            rows = pl.ds(f * 16 + (i >> 3) * 8, 8)
            packed = pltpu.roll(top_in[sweep, part, rows, :], (128 - (i & 7) * 16) & 127, 1)
            for first, last in runs:
                inner = slice(8 + 8 * first, 8 + 8 * last)
                own = fields[field][f, i + 1, inner, :]
                peer = jnp.concatenate(
                    [packed if n == 0 else pltpu.roll(packed, 128 - n, 1) for n in range(first, last)], axis=0
                )
                rate = exchange[i, 8 * first : 8 * last, :]
                if transposed:
                    value = own - rate * (own_share * own - peer_share * peer)
                else:
                    value = own - rate * (own_share * (own - peer))
                fields[field][f, i + 1, inner, :] = value

    def vertical(here):
        above = jnp.where(lane == 127, here, pltpu.roll(here, 127, 1))
        below = jnp.where(lane == 0, here, pltpu.roll(here, 1, 1))
        return 0.3 * here + 0.15 * (above + below)

    def neighbourhood(field, f, i, low):
        here = field[f, i + 1, low : low + BLOCK, :]
        up = field[f, i + 2, low : low + BLOCK, :]
        down = field[f, i, low : low + BLOCK, :]
        right = field[f, i + 1, low + 1 : low + 1 + BLOCK, :]
        left = field[f, i + 1, low - 1 : low - 1 + BLOCK, :]
        return here, up, down, right, left

    def tangent_row(sweep, target, i):
        for block in range(128 // BLOCK):
            low = 8 + block * BLOCK
            u = wind_x[i + 1, block * BLOCK : (block + 1) * BLOCK, :]
            w = wind_y[i, low : low + BLOCK, :]
            for f in range(2):
                here, up, down, right, left = neighbourhood(fields[sweep], f, i, low)
                fields[target][f, i + 1, low : low + BLOCK, :] = (
                    vertical(here) + 0.1 * ((up + down) + (right + left)) - (u * (up - down) + w * (right - left))
                )

    def adjoint_row(sweep, target, i):
        for block in range(128 // BLOCK):
            low = 8 + block * BLOCK
            inner = slice(block * BLOCK, (block + 1) * BLOCK)
            from_down = 0.1 - wind_x[i, inner, :]
            from_up = 0.1 + wind_x[i + 2, inner, :]
            from_left = 0.1 - wind_y[i, low - 1 : low - 1 + BLOCK, :]
            from_right = 0.1 + wind_y[i, low + 1 : low + 1 + BLOCK, :]
            for f in range(2):
                here, up, down, right, left = neighbourhood(fields[sweep], f, i, low)
                fields[target][f, i + 1, low : low + BLOCK, :] = (
                    vertical(here) + (from_down * down + from_up * up) + (from_left * left + from_right * right)
                )

    def each(body, low=0, high=16):
        def step(i, _):
            body(i)
            return 0

        lax.fori_loop(low, high, step, 0, unroll=4 if (high - low) % 4 == 0 else 7)

    for load in loads[:4]:
        load.wait()
    owner = owner_ref[...]
    owner_gx, owner_gy = owner >> 4, owner & 15
    owner_x, owner_y, owner_z = owner_gy >> 2, owner_gx >> 1, ((owner_gy & 3) << 1) | (owner_gx & 1)
    relative = ((owner_y - y + 4) & 3) * 32 + ((owner_x - x + 4) & 3) * 8 + ((owner_z - z + 8) & 7)
    tile_iota = lax.broadcasted_iota(jnp.int32, (128, 512), 0)
    hits = jnp.where(tile_iota == relative, 1.0, 0.0)
    hits_narrow = hits.astype(BF16)
    earlier = jnp.where(
        lax.broadcasted_iota(jnp.int32, (512, 512), 0) < lax.broadcasted_iota(jnp.int32, (512, 512), 1), 1.0, 0.0
    ).astype(BF16)
    slot = jnp.sum(matmul(hits_narrow, earlier) * hits, axis=0, keepdims=True).astype(jnp.int32)
    position = relative * 8 + slot
    column = column_ref[...]
    in_row = tile_iota == (relative & 15) * 8 + slot
    column_high = jnp.where(in_row, (column >> 7).astype(F32), 0.0).astype(BF16)
    column_low = jnp.where(in_row, (column & 127).astype(F32), 0.0).astype(BF16)
    send[:, 16, :] = 128.0 * matmul_nt(hits_narrow, column_high) + matmul_nt(hits_narrow, column_low)
    scale_high, scale_low = split(jnp.broadcast_to(jnp.sqrt(prec_ref[...]), (128, 512)))
    ops_high, ops_low = split(ops[...])

    def pack(chunk, _):
        slots = lax.broadcasted_iota(jnp.int32, (256, 512), 0) + chunk * 256
        pick = jnp.where(slots == position, 1.0, 0.0).astype(BF16)
        scale = matmul_nt(pick, scale_high) + matmul_nt(pick, scale_low)
        rows = matmul(pick, ops_high) + matmul(pick, ops_low)
        target = pl.ds(chunk * GROUP, GROUP)
        send[target, 0:8, :] = (rows[:, :128] * scale).reshape(GROUP, 8, 128)
        send[target, 8:16, :] = (rows[:, 128:] * scale).reshape(GROUP, 8, 128)
        return 0

    lax.fori_loop(0, CHUNKS, pack, 0)

    top_out[...] = jnp.zeros((4, 2, 32, 128), F32)
    for flat in flat_fields:
        for f in range(2):
            for j in (-1, 128):
                flat[edge_row(f, j), :] = jnp.zeros((16, 128), F32)

    loads[4].wait()

    def turn_state(i):
        for f in range(2):
            field_0[f, i + 1, 8:136, :] = flat_native[pl.ds(f * 2048 + i, 128, stride=16), :].T

    pl.semaphore_wait(barrier, 27)
    for step in range(1, 8):
        greet(line_sem, device(x, y, (z + step) & 7))
    each(turn_state)
    first_halo = start_tangent_halo(0)
    pl.semaphore_wait(line_sem, 7)

    pltpu.make_async_copy(send.at[0], recv.at[0], a2a_recv.at[0]).start()

    def dispatch(s, _):
        target = device((x + ((s >> 3) & 3)) & 3, (y + (s >> 5)) & 3, (z + (s & 7)) & 7)
        pltpu.make_async_remote_copy(
            send.at[s], recv.at[s], a2a_send, a2a_recv.at[s >> 5], device_id=target, device_id_type=MESH,
        ).start()
        return 0

    lax.fori_loop(1, 32, dispatch, 0)

    loads[5].wait()
    loads[6].wait()
    loads[7].wait()
    wind_x[0] = jnp.full((128, 128), -0.9, F32)
    wind_x[17] = jnp.full((128, 128), 0.9, F32)

    def turn_winds(i):
        wind_x[i + 1] = 0.5 * flat_winds[pl.ds(i, 128, stride=16), :].T
        wind_y[i, 8:136, :] = 0.5 * flat_winds[pl.ds(2048 + i, 128, stride=16), :].T
        wind_y[i, 0:8, :] = jnp.full((8, 128), -0.9, F32)
        wind_y[i, 136:144, :] = jnp.full((8, 128), 0.9, F32)
        rate = jnp.broadcast_to(gamma_ref[pl.ds(i, 1), :], (128, 128)).T
        exchange[i] = jnp.where(lax.broadcasted_iota(jnp.int32, (128, 128), 1) == 0, rate, 0.0)

    each(turn_winds)

    tops = []

    def sweep_rows(sweep, copies, compute, target, meet, after):
        each(compute, 1, 15)
        copies[2].wait_recv()
        copies[3].wait_recv()
        add_lanes(sweep, target, 0, 16)
        if meet is not None:
            each(lambda i: pack_top(meet, 0, target, i), 1, 15)
            inner = top_copy(meet, 0)
            inner.start()
            tops.append(inner)
            inner.wait_recv()
        each(lambda i: after(i, 0), 1, 15)
        take_rows(sweep, copies)
        for i in (0, 15):
            compute(i)
            add_lanes(sweep, target, i, 1)
            if meet is not None:
                pack_top(meet, 1, target, i)
        if meet is not None:
            outer = top_copy(meet, 1)
            outer.start()
            tops.append(outer)
            outer.wait_recv()
        for i in (0, 15):
            after(i, 1)

    precision = [jnp.broadcast_to(precision_ref[f : f + 1, :], (128, 128)).T for f in range(2)]

    def scale_state(i):
        for f in range(2):
            rows = pl.ds(f * 2048 + i, 128, stride=16)
            flat_out[rows, :] = precision[f] * flat_native[rows, :]

    each(scale_state)
    sweep_rows(
        0, first_halo, lambda i: tangent_row(0, 1, i), 1, 0, lambda i, part: couple(0, part, 1, i, False)
    )
    second_halo = start_tangent_halo(1)
    lax.fori_loop(32, 128, dispatch, 0, unroll=4)

    def finish_second(i, part):
        couple(1, part, 2, i, False)
        for f in range(2):
            high, low = split(field_2[f, i + 1, 8:136, :])
            second[pl.ds(i * 128, 128), 128 * f : 128 * f + 128] = high
            second[pl.ds(i * 128, 128), 256 + 128 * f : 384 + 128 * f] = low
            field_2[f, i + 1, 8:136, :] = jnp.zeros((128, 128), F32)

    sweep_rows(1, second_halo, lambda i: tangent_row(1, 2, i), 2, 1, finish_second)
    for copy in second_halo:
        copy.wait_send()

    def observe(chunk, _):
        arrived = recv.at[pl.ds(chunk * GROUP, GROUP)]
        pltpu.make_async_copy(arrived, arrived, a2a_recv.at[chunk]).wait()
        group = pl.ds(chunk * GROUP, GROUP)
        where = jnp.concatenate(
            [
                jnp.sum(recv[pl.ds(chunk * GROUP, 16), 16, :], axis=0, keepdims=True),
                jnp.sum(recv[pl.ds(chunk * GROUP + 16, 16), 16, :], axis=0, keepdims=True),
            ],
            axis=1,
        ).astype(jnp.int32)
        down_rows = jnp.broadcast_to(where, (128, 256)).T
        within = lax.broadcasted_iota(jnp.int32, (256, 128), 1)
        for i in range(16):
            pick_cell[:, 128 * i : 128 * i + 128] = jnp.where(down_rows == within + 128 * i, 1.0, 0.0).astype(BF16)
        both = matmul(pick_cell[...], second[...])
        sampled = both[:, :256] + both[:, 256:]
        weights = jnp.concatenate(
            [recv[group, 0:8, :].reshape(256, 128), recv[group, 8:16, :].reshape(256, 128)], axis=1
        )
        spread = jnp.concatenate(split(weights * jnp.sum(sampled * weights, axis=1, keepdims=True)), axis=0)

        def scatter(quarter):
            cell = lax.broadcasted_iota(jnp.int32, (512, 256), 0) + quarter * 512
            pick = jnp.where(cell == where, 1.0, 0.0).astype(BF16)
            added = matmul(jnp.concatenate([pick, pick], axis=1), spread)
            for r in range(4):
                for f in range(2):
                    field_2[f, quarter * 4 + r + 1, 8:136, :] += added[
                        128 * r : 128 * r + 128, 128 * f : 128 * f + 128
                    ]

        each(scatter, 0, 4)
        return 0

    lax.fori_loop(0, CHUNKS, observe, 0)

    def start_adjoint_halo(sweep):
        copies = halo_copies(sweep, (row_out.at[sweep - 2, 0], row_out.at[sweep - 2, 1]))
        right = 0.1 - flat_wind_y[pl.ds(8 + 127, 16, stride=PAD), :]
        left = 0.1 + flat_wind_y[pl.ds(8, 16, stride=PAD), :]
        for f in range(2):
            lane_out[sweep, 0, 16 * f : 16 * f + 16, :] = right * flat_fields[sweep][edge_row(f, 127), :]
            lane_out[sweep, 1, 16 * f : 16 * f + 16, :] = left * flat_fields[sweep][edge_row(f, 0), :]
        copies[2].start()
        copies[3].start()
        for f in range(2):
            row_out[sweep - 2, 0, f] = (0.1 - wind_x[16]) * fields[sweep][f, 16, 8:136, :]
        copies[0].start()
        for f in range(2):
            row_out[sweep - 2, 1, f] = (0.1 + wind_x[1]) * fields[sweep][f, 1, 8:136, :]
        copies[1].start()
        return copies

    for i in (0, 15):
        pack_top(2, 1, 2, i)
    each(lambda i: pack_top(2, 1, 2, i, (0, 15)), 1, 15)
    outer_top = top_copy(2, 1)
    outer_top.start()
    each(lambda i: pack_top(2, 0, 2, i, range(1, 15)), 1, 15)
    inner_top = top_copy(2, 0)
    inner_top.start()
    outer_top.wait_recv()
    for i in (0, 15):
        couple(2, 1, 2, i, True)
    each(lambda i: couple(2, 1, 2, i, True, ((0, 1), (15, 16))), 1, 15)
    third_halo = start_adjoint_halo(2)
    inner_top.wait_recv()
    each(lambda i: couple(2, 0, 2, i, True, ((1, 8), (8, 15))), 1, 15)
    sweep_rows(2, third_halo, lambda i: adjoint_row(2, 3, i), 3, 3, lambda i, part: couple(3, part, 3, i, True))
    fourth_halo = start_adjoint_halo(3)

    def turn_back(i, part):
        for f in range(2):
            rows = pl.ds(f * 2048 + i, 128, stride=16)
            flat_out[rows, :] = flat_out[rows, :] + field_1[f, i + 1, 8:136, :].T

    sweep_rows(3, fourth_halo, lambda i: adjoint_row(3, 1, i), 1, None, turn_back)
    started = tops + [outer_top, inner_top] + first_halo + third_halo + fourth_halo
    for copy in started:
        copy.wait_send()
    sent = recv.at[pl.ds(1, 127)]
    pltpu.make_async_copy(sent, sent, a2a_send).wait()


def local(state_incr, winds, coupling, background, obs_dest, obs_col, obs_op, obs_prec):
    shape = state_incr.shape[1:]
    tile = (shape[0] * shape[1],) + shape[2:]
    hbm = pl.BlockSpec(memory_space=pltpu.HBM)
    result = pl.pallas_call(
        kernel,
        out_shape=pltpu.VMEM(tile, F32),
        in_specs=[hbm] * 8,
        out_specs=pl.BlockSpec(memory_space=pltpu.VMEM),
        scratch_shapes=[
            pltpu.VMEM((1, 512), jnp.int32),
            pltpu.VMEM((1, 512), jnp.int32),
            pltpu.VMEM((1, 512), F32),
            pltpu.VMEM((16, 128), F32),
            pltpu.VMEM((2, 128), F32),
            pltpu.VMEM(tile, F32),
            pltpu.VMEM(tile, F32),
            pltpu.VMEM((2, 18, PAD, 128), F32),
            pltpu.VMEM((2, 18, PAD, 128), F32),
            pltpu.VMEM((2, 18, PAD, 128), F32),
            pltpu.VMEM((2, 18, PAD, 128), F32),
            pltpu.VMEM((18, 128, 128), F32),
            pltpu.VMEM((16, PAD, 128), F32),
            pltpu.VMEM((16, 128, 128), F32),
            pltpu.VMEM((512, 256), F32),
            pltpu.VMEM((128, 17, 128), F32),
            pltpu.VMEM((128, 17, 128), F32),
            pltpu.VMEM((2, 2, 2, 128, 128), F32),
            pltpu.VMEM((4, 2, 32, 128), F32),
            pltpu.VMEM((4, 2, 32, 128), F32),
            pltpu.VMEM((4, 2, 32, 128), F32),
            pltpu.VMEM((4, 2, 32, 128), F32),
            pltpu.VMEM((2048, 512), BF16),
            pltpu.VMEM((256, 2048), BF16),
            pltpu.SemaphoreType.DMA((8,)),
            pltpu.SemaphoreType.DMA,
            pltpu.SemaphoreType.DMA((CHUNKS,)),
            pltpu.SemaphoreType.DMA((4, 4)),
            pltpu.SemaphoreType.DMA((4, 4)),
            pltpu.SemaphoreType.DMA((4, 2)),
            pltpu.SemaphoreType.DMA((4, 2)),
            pltpu.SemaphoreType.REGULAR,
        ],
        compiler_params=pltpu.CompilerParams(
            collective_id=0, has_side_effects=True, vmem_limit_bytes=60 * 1024 * 1024
        ),
    )(
        state_incr.reshape(tile), winds.reshape(tile), obs_op,
        obs_dest.reshape(1, -1), obs_col.reshape(1, -1), obs_prec.reshape(1, -1), coupling, background[0],
    )
    return result.reshape((1,) + shape)


def solution(mesh):
    placed = (
        P("comp", None, None, "gx", "gy"),
        P("comp", None, None, "gx", "gy"),
        P("gx", "gy"),
        P("comp", None, None),
        P(("comp", "gx", "gy"), None),
        P(("comp", "gx", "gy")),
        P(("comp", "gx", "gy"), None),
        P(("comp", "gx", "gy")),
    )
    return jax.shard_map(
        local,
        mesh=mesh,
        in_specs=placed,
        out_specs=P("comp", None, None, "gx", "gy"),
        check_vma=False,
    )
```
